256 devices in a mesh: box: 32 (over y, z_lo, x), row: 8 (over z_hi, core).
Axes of the slice: x: 4, y: 4, z: 8 (z_hi: 4, z_lo: 2; z = z_hi * 2 + z_lo), core: 2. Of those that a mesh axis runs over, the one named last changes fastest.
Arguments:
- dtn_map: float32 [64, 4, 128, 512], P('box', None, 'row'), as said below
- boundary_data: bfloat16 [64, 3, 128, 768], P('box'), may hold values from -6 to 6
- solution_op: bfloat16 [64, 16384, 512], P('box', 'row'), may hold values from -0.25 to 0.25
Outputs:
- parent_map: float32 [64, 3, 128, 768], P('box', None, 'row')
- interior_field: bfloat16 [64, 16384, 768], P('box', 'row')
The draws below stay inside these ranges and needn't reach their ends.
Inputs may be any that keep to these rules, and one draw needn't show every extreme that they name: `dtn_map`: in the 128 x 128 block that couples each side with itself, every map is symmetric and its diagonal exceeds the sum of the magnitudes of the rest of the block's row by 0.1 or more.
All inputs are finite; a program needn't handle non-finite values.
Results may differ from the reference program's by a relative error of at most 0.0027.
Values may be sent and summed in bfloat16 or wider, within the bound.
No kernel may reach another device: no remote copies, remote signals or barrier semaphores. Data moves between devices by JAX's collectives and lax.ppermute only.
A program may use at most 64 MiB of HBM per device.

```python
import math
import jax
import jax.numpy as jnp
from jax import lax

EDGE = 128
BOX_DEV = 2
LOADS = 768
BOXES = 64
INTERIOR = 16384
N_BOX = 32


def draw_dtn_map(key, part):
    key_cross, key_size, key_diag, key_signs = jax.random.split(key, 4)
    array_dims = (BOXES, 4, EDGE, 4 * EDGE)
    cross = jnp.clip(jax.random.normal(key_cross, array_dims, jnp.float32), -4.0, 4.0) * (1.15 / math.sqrt(EDGE))
    diagonal = jnp.exp(jax.random.uniform(key_diag, (BOXES, 4, EDGE), jnp.float32, math.log(1.4), math.log(2.8)))
    magnitude = jax.random.uniform(key_size, (BOXES, 4, EDGE, EDGE), jnp.float32, 0.5, 1.0)
    signs = jnp.where(jax.random.bernoulli(key_signs, 0.5, (BOXES, 4, EDGE, EDGE)), 1.0, -1.0)
    signed = magnitude * signs
    symmetric = 0.5 * (signed + jnp.swapaxes(signed, -1, -2))
    points = jnp.arange(EDGE).astype(jnp.float32)
    distance = jnp.abs(points[:, None] - points[None, :])
    falloff = jnp.where(distance > 0.0, 1.0 / ((1.0 + distance) * (1.0 + distance)), 0.0)
    block = symmetric * falloff + diagonal[..., None] * jnp.eye(EDGE, dtype=jnp.float32)
    tiled = jnp.tile(block, (1, 1, 1, 4))
    column_side = jnp.arange(4 * EDGE) // EDGE
    row_side = jnp.arange(4)
    same_side = row_side[:, None, None] == column_side[None, None, :]
    return jnp.where(same_side, tiled, cross).astype(jnp.float32)


def block_levels(stream_key, shape, shards, smallest, largest):
    loudness, own = 1.0, jax.random.fold_in(stream_key, 6)
    for position, parts in shards:
        heights = jnp.exp(jax.random.uniform(jax.random.fold_in(own, position), (parts,), jnp.float32, smallest / len(shards), largest / len(shards)))
        loudness = loudness * jnp.repeat(heights, shape[position] // parts).reshape([-1 if axis == position else 1 for axis in range(len(shape))])
    return loudness


def normal_values(rng, dims, spread, limit, pieces=(), kind=jnp.bfloat16):
    values = spread * jax.random.normal(rng, dims, jnp.float32)
    if pieces:
        values = values * block_levels(rng, dims, pieces, -0.22, 0.18)
    return jnp.clip(values, -limit, limit).astype(kind)


def setup_inputs(seed: int = 0) -> dict:
    key_list = jax.random.split(jax.random.key(seed), 4)
    return {
        "dtn_map": draw_dtn_map(jax.random.fold_in(key_list[3], 71), 0),
        "boundary_data": normal_values(key_list[1], (BOXES, 3, EDGE, LOADS), 1.0, 6.0, ((0, 32),)),
        "solution_op": normal_values(key_list[2], (BOXES, INTERIOR, 4 * EDGE), (4 * EDGE) ** -0.5, 0.25, ((0, 32), (1, 8))),
    }


def invert_factor(factor):
    identity = jnp.eye(factor.shape[0], dtype=jnp.float32)
    return lax.linalg.triangular_solve(factor, identity, left_side=True, lower=True)

def solve_shared(inverse_factor, right_side):
    highest = lax.Precision.HIGHEST
    lower_part = jnp.dot(inverse_factor, right_side, precision=highest)
    return jnp.dot(inverse_factor.T, lower_part, precision=highest)

def merge_pair(inputs):
    alpha_map, beta_map, alpha_data, beta_data, alpha_solver, beta_solver = inputs
    edge_size = alpha_map.shape[1]
    outer_size = 3 * edge_size
    highest = lax.Precision.HIGHEST
    shared_block = alpha_map[3, :, outer_size:] + beta_map[3, :, outer_size:]
    factor = jnp.linalg.cholesky(shared_block)
    inverse_factor = invert_factor(factor)
    coupling = jnp.concatenate([alpha_map[3, :, :outer_size], beta_map[3, :, :outer_size]], axis=1)
    transfer = -solve_shared(inverse_factor, coupling)
    alpha_rows = alpha_map[:3].reshape(outer_size, 4 * edge_size)
    beta_rows = beta_map[:3].reshape(outer_size, 4 * edge_size)
    blank_block = jnp.zeros((outer_size, outer_size), jnp.float32)
    alpha_parent = jnp.concatenate([alpha_rows[:, :outer_size], blank_block], axis=1) + jnp.dot(alpha_rows[:, outer_size:], transfer, precision=highest)
    beta_parent = jnp.concatenate([blank_block, beta_rows[:, :outer_size]], axis=1) + jnp.dot(beta_rows[:, outer_size:], transfer, precision=highest)
    alpha_terms = jnp.dot(alpha_map[3, :, :outer_size], alpha_data.astype(jnp.float32), precision=highest)
    beta_terms = jnp.dot(beta_map[3, :, :outer_size], beta_data.astype(jnp.float32), precision=highest)
    edge_values = (-solve_shared(inverse_factor, alpha_terms + beta_terms)).astype(jnp.bfloat16)
    alpha_inner = jnp.dot(alpha_solver.astype(jnp.float32), jnp.concatenate([alpha_data, edge_values], axis=0).astype(jnp.float32), preferred_element_type=jnp.float32).astype(jnp.bfloat16)
    beta_inner = jnp.dot(beta_solver.astype(jnp.float32), jnp.concatenate([beta_data, edge_values], axis=0).astype(jnp.float32), preferred_element_type=jnp.float32).astype(jnp.bfloat16)
    return (jnp.stack([alpha_parent, beta_parent]), jnp.stack([alpha_inner, beta_inner]))

def reference(dtn_map, boundary_data, solution_op):
    halves = N_BOX // 2
    all_maps = dtn_map.reshape(halves, 2, BOX_DEV, 4, EDGE, 4 * EDGE)
    all_data = boundary_data.reshape(halves, 2, BOX_DEV, 3 * EDGE, LOADS)
    operators = solution_op.reshape(halves, 2, BOX_DEV, INTERIOR, 4 * EDGE)
    pairs = halves * BOX_DEV
    inputs = (all_maps[:, 0].reshape(pairs, 4, EDGE, 4 * EDGE), all_maps[:, 1].reshape(pairs, 4, EDGE, 4 * EDGE), all_data[:, 0].reshape(pairs, 3 * EDGE, LOADS), all_data[:, 1].reshape(pairs, 3 * EDGE, LOADS), operators[:, 0].reshape(pairs, INTERIOR, 4 * EDGE), operators[:, 1].reshape(pairs, INTERIOR, 4 * EDGE))
    parents, inners = lax.map(merge_pair, inputs)
    parents = jnp.swapaxes(parents.reshape(halves, BOX_DEV, 2, 3 * EDGE, 6 * EDGE), 1, 2)
    inners = jnp.swapaxes(inners.reshape(halves, BOX_DEV, 2, INTERIOR, LOADS), 1, 2)
    parent_map = parents.reshape(BOXES, 3, EDGE, 6 * EDGE)
    interior_field = inners.reshape(BOXES, INTERIOR, LOADS)
    return (parent_map, interior_field)
```

```python
import functools

import jax
import jax.numpy as jnp
from jax import lax
from jax.experimental import pallas as pl
from jax.experimental.pallas import tpu as pltpu
from jax.sharding import PartitionSpec as P

HIGHEST = lax.Precision.HIGHEST
F32 = jnp.float32
BF16 = jnp.bfloat16
REMAINDER = 2.0**-27
MOST_DOUBLINGS = 40


def from_partner(value):
    pairs = [(source, source ^ 1) for source in range(lax.axis_size("box"))]
    return lax.ppermute(value, "box", pairs)


def dot(left, right, precision=None):
    return jnp.dot(left, right, precision=precision, preferred_element_type=F32)


def invert_kernel(edge, side_ref, gathered_ref, map_ref, inverse_ref, parent_ref, sums, powers):
    boxes = inverse_ref.shape[0]
    outer = 3 * edge
    row = lax.broadcasted_iota(jnp.int32, (edge, edge), 0)
    column = lax.broadcasted_iota(jnp.int32, (edge, edge), 1)
    diagonal = row == column
    norm = jnp.zeros((1, 1), F32)
    for b in range(boxes):
        shared = gathered_ref[:, b, :, :edge].reshape(edge, edge)
        kept = jnp.where(diagonal, shared, 0.0)
        scale = 1.0 / jnp.sum(kept, axis=1, keepdims=True)
        power = jnp.where(diagonal, 0.0, -shared) * scale
        norm = jnp.maximum(norm, jnp.max(jnp.sum(jnp.abs(power), axis=1, keepdims=True), axis=0, keepdims=True))
        sums[b] = jnp.where(diagonal, 1.0, 0.0)
        powers[b] = power

    def more(carry):
        bound, count = carry
        return jnp.logical_and(bound > REMAINDER, count < MOST_DOUBLINGS)

    def square(carry):
        bound, count = carry
        return bound * bound, count + 1

    _, doublings = lax.while_loop(more, square, (norm[0, 0], jnp.int32(0)))

    def double(_, carry):
        for b in range(boxes):
            power = powers[b]
            both = dot(jnp.concatenate([sums[b], power], axis=0), power, HIGHEST)
            sums[b] = sums[b] + both[:edge]
            powers[b] = both[edge:]
        return carry

    lax.fori_loop(0, doublings, double, 0)
    is_alpha = side_ref[0] == 0
    for b in range(boxes):
        shared = gathered_ref[:, b, :, :edge].reshape(edge, edge)
        scale = 1.0 / jnp.sum(jnp.where(diagonal, shared, 0.0), axis=0, keepdims=True)
        inverse = sums[b] * scale
        inverse_ref[b] = inverse
        rows = map_ref[b, :3].reshape(-1, 4 * edge)
        weights = dot(rows[:, outer:], inverse, HIGHEST)
        coupling = gathered_ref[:, b, :, edge:].reshape(edge, 2 * outer)
        change = dot(weights, coupling, HIGHEST)
        own = (rows[:, :outer] - change[:, :outer]).reshape(3, -1, outer)
        other = (-change[:, outer:]).reshape(3, -1, outer)

        @pl.when(is_alpha)
        def _():
            parent_ref[b, :, :, :outer] = own
            parent_ref[b, :, :, outer:] = other

        @pl.when(jnp.logical_not(is_alpha))
        def _():
            parent_ref[b, :, :, :outer] = other
            parent_ref[b, :, :, outer:] = own


def split_three(value):
    first = value.astype(BF16)
    rest = value - first.astype(F32)
    second = rest.astype(BF16)
    third = (rest - second.astype(F32)).astype(BF16)
    return jnp.concatenate([first, second, third], axis=0)


def field_kernel(edge, gathered_ref, inverse_ref, own_ref, other_ref, operator_ref, field_ref, pressure):
    outer = 3 * edge

    @pl.when(pl.program_id(1) == 0)
    def _():
        own = own_ref[0]
        coupling = gathered_ref[:, 0, :, edge:].reshape(edge, 2 * outer)
        parts = dot(split_three(coupling[:, :outer]), own)
        parts += dot(split_three(coupling[:, outer:]), other_ref[0])
        terms = parts[:edge] + (parts[edge : 2 * edge] + parts[2 * edge :])
        pressure[:outer] = own
        pressure[outer:] = (-dot(inverse_ref[0], terms, HIGHEST)).astype(BF16)

    field_ref[0] = dot(operator_ref[0], pressure[...]).astype(BF16)


def per_device(dtn_map, boundary_data, solution_op):
    boxes, _, local, points = dtn_map.shape
    edge = boundary_data.shape[2]
    loads = boundary_data.shape[3]
    cells = solution_op.shape[1]
    outer = 3 * edge
    side = (lax.axis_index("box") % 2).astype(jnp.int32).reshape(1)
    own_rows = dtn_map[:, 3]
    own_data = boundary_data.reshape(boxes, outer, loads)
    other_rows = from_partner(own_rows)
    own_data, started = lax.optimization_barrier((own_data, own_rows))
    other_data = from_partner(own_data)
    packed = jnp.concatenate(
        [
            own_rows[:, :, outer:] + other_rows[:, :, outer:],
            own_rows[:, :, :outer],
            other_rows[:, :, :outer],
        ],
        axis=2,
    )
    gathered = lax.all_gather(packed, "row", axis=0)
    inverse, parent_map = pl.pallas_call(
        functools.partial(invert_kernel, edge),
        out_shape=(
            jax.ShapeDtypeStruct((boxes, edge, edge), F32),
            jax.ShapeDtypeStruct((boxes, 3, local, 2 * outer), F32),
        ),
        in_specs=[
            pl.BlockSpec(memory_space=pltpu.SMEM),
            pl.BlockSpec(memory_space=pltpu.VMEM),
            pl.BlockSpec(memory_space=pltpu.VMEM),
        ],
        out_specs=(
            pl.BlockSpec(memory_space=pltpu.VMEM),
            pl.BlockSpec(memory_space=pltpu.VMEM),
        ),
        scratch_shapes=[
            pltpu.VMEM((boxes, edge, edge), F32),
            pltpu.VMEM((boxes, edge, edge), F32),
        ],
        compiler_params=pltpu.CompilerParams(vmem_limit_bytes=16 << 20),
        name="invert",
    )(side, gathered, dtn_map)
    step = 512
    groups = gathered.shape[0]
    interior_field = pl.pallas_call(
        functools.partial(field_kernel, edge),
        grid=(boxes, cells // step),
        out_shape=jax.ShapeDtypeStruct((boxes, cells, loads), BF16),
        in_specs=[
            pl.BlockSpec((groups, 1, local, gathered.shape[3]), lambda b, i: (0, b, 0, 0)),
            pl.BlockSpec((1, edge, edge), lambda b, i: (b, 0, 0)),
            pl.BlockSpec((1, outer, loads), lambda b, i: (b, 0, 0)),
            pl.BlockSpec((1, outer, loads), lambda b, i: (b, 0, 0)),
            pl.BlockSpec((1, step, points), lambda b, i: (b, i, 0)),
        ],
        out_specs=pl.BlockSpec((1, step, loads), lambda b, i: (b, i, 0)),
        scratch_shapes=[pltpu.VMEM((points, loads), BF16)],
        compiler_params=pltpu.CompilerParams(vmem_limit_bytes=32 << 20),
        name="field",
    )(gathered, inverse, own_data, other_data, solution_op)
    return (parent_map, interior_field)


def solution(mesh):
    in_specs = (P("box", None, "row", None), P("box", None, None, None), P("box", "row", None))
    out_specs = (P("box", None, "row", None), P("box", "row", None))
    return jax.shard_map(
        per_device, mesh=mesh, in_specs=in_specs, out_specs=out_specs, check_vma=False
    )
```

```python
import functools

import jax
import jax.numpy as jnp
from jax import lax
from jax.experimental import pallas as pl
from jax.experimental.pallas import tpu as pltpu
from jax.sharding import PartitionSpec as P

HIGHEST = lax.Precision.HIGHEST
F32 = jnp.float32
BF16 = jnp.bfloat16
REMAINDER = 2.0**-27
MOST_DOUBLINGS = 40


def exchange(value, axis):
    pairs = [(source, source ^ 1) for source in range(lax.axis_size(axis))]
    return lax.ppermute(value, axis, pairs)


def dot(left, right, precision=None):
    return jnp.dot(left, right, precision=precision, preferred_element_type=F32)


def invert_kernel(edge, place_ref, gathered_ref, map_ref, inverse_ref, parent_ref, sums, powers):
    boxes = inverse_ref.shape[0]
    outer = 3 * edge
    row = lax.broadcasted_iota(jnp.int32, (edge, edge), 0)
    column = lax.broadcasted_iota(jnp.int32, (edge, edge), 1)
    diagonal = row == column
    norm = jnp.zeros((1, 1), F32)
    for b in range(boxes):
        shared = gathered_ref[:, b, :, :edge].reshape(edge, edge)
        kept = jnp.where(diagonal, shared, 0.0)
        scale = 1.0 / jnp.sum(kept, axis=1, keepdims=True)
        power = jnp.where(diagonal, 0.0, -shared) * scale
        norm = jnp.maximum(norm, jnp.max(jnp.sum(jnp.abs(power), axis=1, keepdims=True), axis=0, keepdims=True))
        sums[b] = jnp.where(diagonal, 1.0, 0.0)
        powers[b] = power

    def more(carry):
        bound, count = carry
        return jnp.logical_and(bound > REMAINDER, count < MOST_DOUBLINGS)

    def square(carry):
        bound, count = carry
        return bound * bound, count + 1

    _, doublings = lax.while_loop(more, square, (norm[0, 0], jnp.int32(0)))

    def double(_, carry):
        for b in range(boxes):
            power = powers[b]
            both = dot(jnp.concatenate([sums[b], power], axis=0), power, HIGHEST)
            sums[b] = sums[b] + both[:edge]
            powers[b] = both[edge:]
        return carry

    lax.fori_loop(0, doublings, double, 0)
    is_alpha = place_ref[0] < 2
    for b in range(boxes):
        shared = gathered_ref[:, b, :, :edge].reshape(edge, edge)
        scale = 1.0 / jnp.sum(jnp.where(diagonal, shared, 0.0), axis=0, keepdims=True)
        inverse = sums[b] * scale
        inverse_ref[b] = inverse
        rows = map_ref[b, :3].reshape(-1, 4 * edge)
        weights = dot(rows[:, outer:], inverse, HIGHEST)
        coupling = gathered_ref[:, b, :, edge:].reshape(edge, 2 * outer)
        change = dot(weights, coupling, HIGHEST)
        own = (rows[:, :outer] - change[:, :outer]).reshape(3, -1, outer)
        other = (-change[:, outer:]).reshape(3, -1, outer)

        @pl.when(is_alpha)
        def _():
            parent_ref[b, :, :, :outer] = own
            parent_ref[b, :, :, outer:] = other

        @pl.when(jnp.logical_not(is_alpha))
        def _():
            parent_ref[b, :, :, :outer] = other
            parent_ref[b, :, :, outer:] = own


def split_three(value):
    first = value.astype(BF16)
    rest = value - first.astype(F32)
    second = rest.astype(BF16)
    third = (rest - second.astype(F32)).astype(BF16)
    return jnp.concatenate([first, second, third], axis=0)


def early_kernel(chunk, place_ref, rows_ref, data_ref, operator_ref, partial_ref, sent_ref, staged, arrived):
    boxes, cells, _ = partial_ref.shape
    depth = staged.shape[2]
    places = [(b, slice(start, start + chunk)) for b in range(boxes) for start in range(0, cells, chunk)]
    copies = [
        pltpu.make_async_copy(
            operator_ref.at[b, cut, pl.ds(0, depth)], staged.at[b, cut], arrived.at[order]
        )
        for order, (b, cut) in enumerate(places)
    ]
    for copy in copies:
        copy.start()
    sent_ref[...] = data_ref[place_ref[0] & 1]
    for copy, (b, cut) in zip(copies, places):
        copy.wait()
        partial_ref[b, cut] = dot(staged[b, cut], data_ref[b, :depth])


def field_kernel(
    edge,
    chunk,
    place_ref,
    gathered_ref,
    inverse_ref,
    own_ref,
    crossed_ref,
    sibling_ref,
    partial_ref,
    operator_ref,
    field_ref,
    staged,
    pressure,
    finished,
    arrived,
    left,
):
    boxes, cells, _ = partial_ref.shape
    outer = 3 * edge
    depth = staged.shape[2]
    core = place_ref[0] & 1
    order = [core if turn == 0 else 1 - core for turn in range(boxes)]
    starts = range(0, cells, chunk)
    count = len(starts)
    reads = [
        pltpu.make_async_copy(
            operator_ref.at[order[turn], pl.ds(start, chunk), pl.ds(depth, depth)],
            staged.at[turn, pl.ds(start, chunk)],
            arrived.at[turn * count + place],
        )
        for turn in range(boxes)
        for place, start in enumerate(starts)
    ]
    for copy in reads:
        copy.start()
    writes = []
    for turn, other_ref in enumerate((crossed_ref, sibling_ref)):
        b = order[turn]
        own = own_ref[b]
        coupling = gathered_ref[:, b, :, edge:].reshape(edge, 2 * outer)
        parts = dot(split_three(coupling[:, :outer]), own)
        parts += dot(split_three(coupling[:, outer:]), other_ref[...])
        terms = parts[:edge] + (parts[edge : 2 * edge] + parts[2 * edge :])
        pressure[: outer - depth] = own[depth:]
        pressure[outer - depth :] = (-dot(inverse_ref[b], terms, HIGHEST)).astype(BF16)
        for place, start in enumerate(starts):
            reads[turn * count + place].wait()
            cut = slice(start, start + chunk)
            total = partial_ref[b, cut] + dot(staged[turn, cut], pressure[...])
            finished[turn, cut] = total.astype(BF16)
            copy = pltpu.make_async_copy(
                finished.at[turn, cut], field_ref.at[b, cut], left.at[turn * count + place]
            )
            copy.start()
            writes.append(copy)
    for copy in writes:
        copy.wait()


def in_vmem(value):
    return pltpu.with_memory_space_constraint(value, pltpu.VMEM)


def in_hbm(value):
    return pltpu.with_memory_space_constraint(value, pltpu.HBM)


SMEM_SPEC = pl.BlockSpec(memory_space=pltpu.SMEM)
VMEM_SPEC = pl.BlockSpec(memory_space=pltpu.VMEM)
HBM_SPEC = pl.BlockSpec(memory_space=pltpu.HBM)
ANY_SPEC = pl.BlockSpec(memory_space=pl.ANY)


def per_device(dtn_map, boundary_data, solution_op):
    boxes, _, local, points = dtn_map.shape
    edge = boundary_data.shape[2]
    loads = boundary_data.shape[3]
    cells = solution_op.shape[1]
    outer = 3 * edge
    depth = points // 2
    side = lax.axis_index("box") & 1
    core = lax.axis_index("row") & 1
    place = (2 * side + core).astype(jnp.int32).reshape(1)
    own_rows = dtn_map[:, 3]
    own_data = boundary_data.reshape(boxes, outer, loads)
    operator = in_hbm(solution_op)
    other_rows = exchange(own_rows, "box")
    chunk = 512
    pieces = boxes * cells // chunk
    partial, sent = pl.pallas_call(
        functools.partial(early_kernel, chunk),
        out_shape=(
            pltpu.VMEM((boxes, cells, loads), F32),
            jax.ShapeDtypeStruct((outer, loads), BF16),
        ),
        in_specs=[SMEM_SPEC, ANY_SPEC, VMEM_SPEC, HBM_SPEC],
        out_specs=(VMEM_SPEC, VMEM_SPEC),
        scratch_shapes=[
            pltpu.VMEM((boxes, cells, depth), BF16),
            pltpu.SemaphoreType.DMA((pieces,)),
        ],
        compiler_params=pltpu.CompilerParams(vmem_limit_bytes=24 << 20),
        cost_estimate=pl.CostEstimate(
            flops=2 * boxes * cells * depth * loads, bytes_accessed=4 << 20, transcendentals=0
        ),
        name="early",
    )(place, own_rows, own_data, operator)
    crossed = exchange(sent, "box")
    packed = jnp.concatenate(
        [
            own_rows[:, :, outer:] + other_rows[:, :, outer:],
            own_rows[:, :, :outer],
            other_rows[:, :, :outer],
        ],
        axis=2,
    )
    gathered = lax.all_gather(packed, "row", axis=0)
    crossed, gathered = lax.optimization_barrier((crossed, gathered))
    sibling = exchange(crossed, "row")
    inverse, parent_map = pl.pallas_call(
        functools.partial(invert_kernel, edge),
        out_shape=(
            jax.ShapeDtypeStruct((boxes, edge, edge), F32),
            jax.ShapeDtypeStruct((boxes, 3, local, 2 * outer), F32),
        ),
        in_specs=[SMEM_SPEC, VMEM_SPEC, VMEM_SPEC],
        out_specs=(VMEM_SPEC, VMEM_SPEC),
        scratch_shapes=[
            pltpu.VMEM((boxes, edge, edge), F32),
            pltpu.VMEM((boxes, edge, edge), F32),
        ],
        compiler_params=pltpu.CompilerParams(vmem_limit_bytes=8 << 20),
        cost_estimate=pl.CostEstimate(flops=4 << 30, bytes_accessed=4 << 20, transcendentals=0),
        name="invert",
    )(place, gathered, dtn_map)
    interior_field = pl.pallas_call(
        functools.partial(field_kernel, edge, chunk),
        out_shape=jax.ShapeDtypeStruct((boxes, cells, loads), BF16),
        in_specs=[SMEM_SPEC] + [VMEM_SPEC] * 6 + [HBM_SPEC],
        out_specs=ANY_SPEC,
        scratch_shapes=[
            pltpu.VMEM((boxes, cells, depth), BF16),
            pltpu.VMEM((depth, loads), BF16),
            pltpu.VMEM((boxes, cells, loads), BF16),
            pltpu.SemaphoreType.DMA((pieces,)),
            pltpu.SemaphoreType.DMA((pieces,)),
        ],
        compiler_params=pltpu.CompilerParams(vmem_limit_bytes=28 << 20),
        name="field",
    )(place, gathered, inverse, own_data, crossed, sibling, in_vmem(partial), operator)
    return (parent_map, interior_field)


def solution(mesh):
    in_specs = (P("box", None, "row", None), P("box", None, None, None), P("box", "row", None))
    out_specs = (P("box", None, "row", None), P("box", "row", None))
    return jax.shard_map(
        per_device, mesh=mesh, in_specs=in_specs, out_specs=out_specs, check_vma=False
    )
```

```python
import functools

import jax
import jax.numpy as jnp
from jax import lax
from jax.experimental import pallas as pl
from jax.experimental.pallas import tpu as pltpu
from jax.sharding import PartitionSpec as P

HIGHEST = lax.Precision.HIGHEST
F32 = jnp.float32
BF16 = jnp.bfloat16
REMAINDER = 2.0**-27
SURE_DOUBLINGS = 4
MOST_DOUBLINGS = 40

SMEM_SPEC = pl.BlockSpec(memory_space=pltpu.SMEM)
VMEM_SPEC = pl.BlockSpec(memory_space=pltpu.VMEM)
HBM_SPEC = pl.BlockSpec(memory_space=pltpu.HBM)
ANY_SPEC = pl.BlockSpec(memory_space=pl.ANY)


def exchange(value, axis):
    pairs = [(source, source ^ 1) for source in range(lax.axis_size(axis))]
    return lax.ppermute(value, axis, pairs)


def dot(left, right, precision=None):
    return jnp.dot(left, right, precision=precision, preferred_element_type=F32)


def in_hbm(value):
    return pltpu.with_memory_space_constraint(value, pltpu.HBM)


def split(value, count):
    pieces = []
    for _ in range(count):
        piece = value.astype(BF16)
        pieces.append(piece)
        value = value - piece.astype(F32)
    return pieces


def split_dot(left, right):
    high, low = split(left, 2)
    right_high, right_low = split(right, 2)
    both = dot(jnp.concatenate([high, low], axis=0), right_high)
    rows = left.shape[0]
    return both[:rows] + (both[rows:] + dot(high, right_low))


def start_kernel(place_ref, map_ref, data_ref, rows_ref, first_ref, arrived):
    copies = (
        pltpu.make_async_copy(map_ref.at[:, 3], rows_ref, arrived.at[0]),
        pltpu.make_async_copy(data_ref.at[place_ref[0] & 1], first_ref, arrived.at[1]),
    )
    for copy in copies:
        copy.start()
    for copy in copies:
        copy.wait()


def early_kernel(
    chunk,
    place_ref,
    first_ref,
    rows_ref,
    map_ref,
    data_ref,
    operator_ref,
    sent_ref,
    outer_ref,
    second_ref,
    near_ref,
    far_ref,
    partial_ref,
    arrived,
):
    mine = place_ref[0] & 1
    cells, loads = partial_ref.shape
    depth = operator_ref.shape[2] // 2
    cuts = [slice(start, start + chunk) for start in range(0, cells, chunk)]
    moves = [(operator_ref.at[mine, cut], near_ref.at[cut]) for cut in cuts]
    moves += [(operator_ref.at[1 - mine, cut], far_ref.at[cut]) for cut in cuts]
    moves += [(data_ref.at[1 - mine], second_ref), (map_ref.at[:, pl.ds(0, 3)], outer_ref)]
    copies = [
        pltpu.make_async_copy(origin, target, arrived.at[order])
        for order, (origin, target) in enumerate(moves)
    ]
    for copy in copies:
        copy.start()
    for copy, cut in zip(copies, cuts):
        copy.wait()
        partial_ref[cut] = dot(near_ref[cut, :depth], first_ref[:depth])
    for copy in copies[len(cuts) :]:
        copy.wait()


def solve_kernel(place_ref, gathered_ref, own_ref, other_ref, solved_ref, sums, power_ref):
    mine = place_ref[0] & 1
    edge = sums.shape[0]
    outer, loads = own_ref.shape
    shared = gathered_ref[:, mine, :, :edge].reshape(edge, edge)
    row = lax.broadcasted_iota(jnp.int32, (edge, edge), 0)
    column = lax.broadcasted_iota(jnp.int32, (edge, edge), 1)
    diagonal = row == column
    kept = jnp.where(diagonal, shared, 0.0)
    scale = 1.0 / jnp.sum(kept, axis=1, keepdims=True)
    right_scale = 1.0 / jnp.sum(kept, axis=0, keepdims=True)
    power = jnp.where(diagonal, 0.0, -shared) * scale
    size = jnp.sum(jnp.abs(power), axis=1, keepdims=True)
    norm = jnp.max(size, axis=0, keepdims=True)[0, 0]

    coupling = gathered_ref[:, mine, :, edge:].reshape(edge, 2 * outer)
    parts = dot(jnp.concatenate(split(coupling[:, :outer], 3), axis=0), own_ref[...])
    parts += dot(jnp.concatenate(split(coupling[:, outer:], 3), axis=0), other_ref[...])
    terms = parts[:edge] + (parts[edge : 2 * edge] + parts[2 * edge :])

    total = jnp.where(diagonal, 1.0, power)
    power = dot(power, power, HIGHEST)
    for _ in range(SURE_DOUBLINGS - 1):
        both = dot(jnp.concatenate([total, power], axis=0), power, HIGHEST)
        total = total + both[:edge]
        power = both[edge:]
    sums[...] = total + dot(total, power, HIGHEST)

    bound = norm
    for _ in range(SURE_DOUBLINGS + 1):
        bound = bound * bound

    @pl.when(bound > REMAINDER)
    def _():
        power_ref[...] = dot(power, power, HIGHEST)

        def more(carry):
            left, count = carry
            return jnp.logical_and(left > REMAINDER, count < MOST_DOUBLINGS)

        def double(carry):
            left, count = carry
            held = power_ref[...]
            both = dot(jnp.concatenate([sums[...], held], axis=0), held, HIGHEST)
            sums[...] = sums[...] + both[:edge]
            power_ref[...] = both[edge:]
            return left * left, count + 1

        lax.while_loop(more, double, (bound, jnp.int32(0)))

    inverse = sums[...] * right_scale
    solved_ref[:, :loads] = (-split_dot(inverse, terms)).astype(BF16)
    for order, piece in enumerate(split(inverse, 3)):
        solved_ref[:, loads + order * edge : loads + (order + 1) * edge] = piece


def field_kernel(turn, chunk, place_ref, gathered_ref, map_ref, solved_ref, data_ref, operator_ref, *refs):
    if turn:
        refs = refs[2:]
    else:
        partial_ref, *refs = refs
    field_ref, parent_ref, pressure, finished, parent, left = refs
    box = place_ref[0] & 1
    if turn:
        box = 1 - box
    outer, loads = data_ref.shape
    edge = solved_ref.shape[0]
    cells, points = operator_ref.shape
    done = 0 if turn else points // 2
    pressure[:outer] = data_ref[...]
    pressure[outer:] = solved_ref[:, :loads]
    writes = []
    for order, start in enumerate(range(0, cells, chunk)):
        cut = slice(start, start + chunk)
        total = dot(operator_ref[cut, done:], pressure[done:])
        if not turn:
            total = total + partial_ref[cut]
        finished[cut] = total.astype(BF16)
        copy = pltpu.make_async_copy(finished.at[cut], field_ref.at[box, cut], left.at[order])
        copy.start()
        writes.append(copy)
    inverse = jnp.zeros((edge, edge), F32)
    for order in (2, 1, 0):
        inverse = inverse + solved_ref[:, loads + order * edge : loads + (order + 1) * edge].astype(F32)
    rows = map_ref[box].reshape(-1, 4 * edge)
    weights = split_dot(rows[:, outer:], inverse)
    coupling = gathered_ref[:, box, :, edge:].reshape(edge, 2 * outer)
    change = split_dot(weights, coupling)
    own = (rows[:, :outer] - change[:, :outer]).reshape(3, -1, outer)
    other = (-change[:, outer:]).reshape(3, -1, outer)
    is_alpha = place_ref[0] < 2

    @pl.when(is_alpha)
    def _():
        parent[:, :, :outer] = own
        parent[:, :, outer:] = other

    @pl.when(jnp.logical_not(is_alpha))
    def _():
        parent[:, :, :outer] = other
        parent[:, :, outer:] = own

    copy = pltpu.make_async_copy(parent, parent_ref.at[box], left.at[len(writes)])
    copy.start()
    writes.append(copy)
    for copy in writes:
        copy.wait()


def per_device(dtn_map, boundary_data, solution_op):
    boxes, _, local, points = dtn_map.shape
    edge = boundary_data.shape[2]
    loads = boundary_data.shape[3]
    cells = solution_op.shape[1]
    outer = 3 * edge
    side = lax.axis_index("box") & 1
    core = lax.axis_index("row") & 1
    place = (2 * side + core).astype(jnp.int32).reshape(1)
    whole_map = in_hbm(dtn_map)
    data = in_hbm(boundary_data.reshape(boxes, outer, loads))
    half = jax.ShapeDtypeStruct((outer, loads), BF16)
    own_rows, first = pl.pallas_call(
        start_kernel,
        out_shape=(jax.ShapeDtypeStruct((boxes, local, points), F32), half),
        in_specs=[SMEM_SPEC, HBM_SPEC, HBM_SPEC],
        out_specs=(VMEM_SPEC, VMEM_SPEC),
        scratch_shapes=[pltpu.SemaphoreType.DMA((2,))],
        compiler_params=pltpu.CompilerParams(vmem_limit_bytes=4 << 20),
        name="start",
    )(place, whole_map, data)
    other_rows = exchange(own_rows, "box")
    chunk = 512
    sent, outer_rows, second, near, far, partial = pl.pallas_call(
        functools.partial(early_kernel, chunk),
        out_shape=(
            half,
            pltpu.VMEM((boxes, 3, local, points), F32),
            pltpu.VMEM((outer, loads), BF16),
            pltpu.VMEM((cells, points), BF16),
            pltpu.VMEM((cells, points), BF16),
            pltpu.VMEM((cells, loads), F32),
        ),
        in_specs=[SMEM_SPEC, VMEM_SPEC, ANY_SPEC, HBM_SPEC, HBM_SPEC, HBM_SPEC],
        out_specs=(VMEM_SPEC,) * 6,
        scratch_shapes=[pltpu.SemaphoreType.DMA((2 * cells // chunk + 2,))],
        input_output_aliases={1: 0},
        compiler_params=pltpu.CompilerParams(vmem_limit_bytes=4 << 20),
        cost_estimate=pl.CostEstimate(
            flops=cells * points * loads, bytes_accessed=6 << 20, transcendentals=0
        ),
        name="early",
    )(place, first, own_rows, whole_map, data, in_hbm(solution_op))
    first = sent
    crossed = exchange(sent, "box")
    packed = jnp.concatenate(
        [
            own_rows[:, :, outer:] + other_rows[:, :, outer:],
            own_rows[:, :, :outer],
            other_rows[:, :, :outer],
        ],
        axis=2,
    )
    gathered = lax.all_gather(packed, "row", axis=0)
    solved = pl.pallas_call(
        solve_kernel,
        out_shape=jax.ShapeDtypeStruct((edge, loads + 3 * edge), BF16),
        in_specs=[SMEM_SPEC] + [VMEM_SPEC] * 3,
        out_specs=VMEM_SPEC,
        scratch_shapes=[pltpu.VMEM((edge, edge), F32), pltpu.VMEM((edge, edge), F32)],
        compiler_params=pltpu.CompilerParams(vmem_limit_bytes=12 << 20),
        name="solve",
    )(place, gathered, first, crossed)
    swapped = exchange(solved, "row")
    outputs = (
        jax.ShapeDtypeStruct((boxes, cells, loads), BF16),
        jax.ShapeDtypeStruct((boxes, 3, local, 2 * outer), F32),
    )

    def field(turn, given, data, operator, extra):
        return pl.pallas_call(
            functools.partial(field_kernel, turn, chunk),
            out_shape=outputs,
            in_specs=[SMEM_SPEC] + [VMEM_SPEC] * 5 + ([ANY_SPEC] * 2 if turn else [VMEM_SPEC]),
            out_specs=(ANY_SPEC, ANY_SPEC),
            scratch_shapes=[
                pltpu.VMEM((points, loads), BF16),
                pltpu.VMEM((cells, loads), BF16),
                pltpu.VMEM((3, local, 2 * outer), F32),
                pltpu.SemaphoreType.DMA((cells // chunk + 1,)),
            ],
            input_output_aliases={6: 0, 7: 1} if turn else {},
            compiler_params=pltpu.CompilerParams(vmem_limit_bytes=16 << 20),
            cost_estimate=pl.CostEstimate(
                flops=2 * cells * points * loads, bytes_accessed=8 << 20, transcendentals=0
            ),
            name="field",
        )(place, gathered, outer_rows, given, data, operator, *extra)

    made = field(0, solved, first, near, (partial,))
    interior_field, parent_map = field(1, swapped, second, far, made)
    return (parent_map, interior_field)


def solution(mesh):
    in_specs = (P("box", None, "row", None), P("box", None, None, None), P("box", "row", None))
    out_specs = (P("box", None, "row", None), P("box", "row", None))
    return jax.shard_map(
        per_device, mesh=mesh, in_specs=in_specs, out_specs=out_specs, check_vma=False
    )
```

```python
import functools

import jax
import jax.numpy as jnp
from jax import lax
from jax.experimental import pallas as pl
from jax.experimental.pallas import tpu as pltpu
from jax.sharding import PartitionSpec as P

F32 = jnp.float32
BF16 = jnp.bfloat16
REMAINDER = 2.0**-27
SURE_DOUBLINGS = 4
MOST_DOUBLINGS = 40

SMEM_SPEC = pl.BlockSpec(memory_space=pltpu.SMEM)
VMEM_SPEC = pl.BlockSpec(memory_space=pltpu.VMEM)
HBM_SPEC = pl.BlockSpec(memory_space=pltpu.HBM)
ANY_SPEC = pl.BlockSpec(memory_space=pl.ANY)


def exchange(value, axis):
    pairs = [(source, source ^ 1) for source in range(lax.axis_size(axis))]
    return lax.ppermute(value, axis, pairs)


def in_hbm(value):
    return pltpu.with_memory_space_constraint(value, pltpu.HBM)


def dot(left, right, precision=None):
    return jnp.dot(left, right, precision=precision, preferred_element_type=F32)


def split(value, count):
    pieces = []
    for _ in range(count):
        piece = value.astype(BF16)
        pieces.append(piece)
        value = value - piece.astype(F32)
    return pieces


def split_dot(left, right):
    high, low = split(left, 2)
    right_high, right_low = split(right, 2)
    both = dot(jnp.concatenate([high, low], axis=0), right_high)
    rows = left.shape[0]
    return both[:rows] + (both[rows:] + dot(high, right_low))


def full_dot(left, right):
    return dot(left, right, lax.Precision.HIGHEST)


def start_copies(copies):
    for copy in copies:
        copy.start()


def finish_copies(copies):
    for copy in copies:
        copy.wait()


def start_kernel(place_ref, map_ref, data_ref, rows_ref, first_ref, arrived):
    copies = (
        pltpu.make_async_copy(map_ref.at[:, 3], rows_ref, arrived.at[0]),
        pltpu.make_async_copy(data_ref.at[place_ref[0] & 1], first_ref, arrived.at[1]),
    )
    start_copies(copies)
    finish_copies(copies)


def early_kernel(place_ref, first_ref, rows_ref, operator_ref, sent_ref, near_ref, partial_ref, arrived):
    depth = operator_ref.shape[2] // 2
    copy = pltpu.make_async_copy(operator_ref.at[place_ref[0] & 1], near_ref, arrived.at[0])
    copy.start()
    copy.wait()
    partial_ref[...] = dot(near_ref[:, :depth], first_ref[:depth])


def solve_kernel(
    place_ref,
    gathered_ref,
    own_ref,
    other_ref,
    map_ref,
    data_ref,
    operator_ref,
    solved_ref,
    outer_ref,
    second_ref,
    far_ref,
    sums,
    power_ref,
    arrived,
):
    mine = place_ref[0] & 1
    copies = (
        pltpu.make_async_copy(operator_ref.at[1 - mine], far_ref, arrived.at[0]),
        pltpu.make_async_copy(data_ref.at[1 - mine], second_ref, arrived.at[1]),
        pltpu.make_async_copy(map_ref.at[:, pl.ds(0, 3)], outer_ref, arrived.at[2]),
    )
    start_copies(copies)
    edge = sums.shape[0]
    outer, loads = own_ref.shape
    shared = gathered_ref[:, mine, :, :edge].reshape(edge, edge)
    row = lax.broadcasted_iota(jnp.int32, (edge, edge), 0)
    column = lax.broadcasted_iota(jnp.int32, (edge, edge), 1)
    diagonal = row == column
    kept = jnp.where(diagonal, shared, 0.0)
    scale = 1.0 / jnp.sum(kept, axis=1, keepdims=True)
    right_scale = 1.0 / jnp.sum(kept, axis=0, keepdims=True)
    power = jnp.where(diagonal, 0.0, -shared) * scale
    size = jnp.sum(jnp.abs(power), axis=1, keepdims=True)
    norm = jnp.max(size, axis=0, keepdims=True)[0, 0]

    coupling = gathered_ref[:, mine, :, edge:].reshape(edge, 2 * outer)
    parts = dot(jnp.concatenate(split(coupling[:, :outer], 2), axis=0), own_ref[...])
    parts += dot(jnp.concatenate(split(coupling[:, outer:], 2), axis=0), other_ref[...])
    terms = parts[:edge] + parts[edge:]

    total = jnp.where(diagonal, 1.0, power)
    power = split_dot(power, power)
    for _ in range(SURE_DOUBLINGS - 1):
        both = split_dot(jnp.concatenate([total, power], axis=0), power)
        total = total + both[:edge]
        power = both[edge:]
    sums[...] = total + split_dot(total, power)

    bound = norm
    for _ in range(SURE_DOUBLINGS + 1):
        bound = bound * bound

    @pl.when(bound > REMAINDER)
    def _():
        power_ref[...] = full_dot(power, power)

        def more(carry):
            left, count = carry
            return jnp.logical_and(left > REMAINDER, count < MOST_DOUBLINGS)

        def double(carry):
            left, count = carry
            held = power_ref[...]
            both = full_dot(jnp.concatenate([sums[...], held], axis=0), held)
            sums[...] = sums[...] + both[:edge]
            power_ref[...] = both[edge:]
            return left * left, count + 1

        lax.while_loop(more, double, (bound, jnp.int32(0)))

    inverse = sums[...] * right_scale
    solved_ref[:, :loads] = (-split_dot(inverse, terms)).astype(BF16)
    for order, piece in enumerate(split(inverse, 3)):
        solved_ref[:, loads + order * edge : loads + (order + 1) * edge] = piece
    finish_copies(copies)


def parent_rows(place_ref, gathered_ref, outer_ref, solved_ref, box, loads):
    edge = solved_ref.shape[0]
    outer = 3 * edge
    inverse = jnp.zeros((edge, edge), F32)
    for order in (2, 1, 0):
        inverse = inverse + solved_ref[:, loads + order * edge : loads + (order + 1) * edge].astype(F32)
    rows = outer_ref[box].reshape(-1, 4 * edge)
    weights = split_dot(rows[:, outer:], inverse)
    coupling = gathered_ref[:, box, :, edge:].reshape(edge, 2 * outer)
    change = split_dot(weights, coupling)
    own = rows[:, :outer] - change[:, :outer]
    other = -change[:, outer:]
    is_alpha = place_ref[0] < 2
    left = jnp.where(is_alpha, own, other)
    right = jnp.where(is_alpha, other, own)
    return jnp.concatenate([left, right], axis=1).reshape(3, -1, 2 * outer)


def middle_kernel(
    place_ref, gathered_ref, outer_ref, solved_ref, second_ref, far_ref, partial_ref, parent_ref
):
    depth = far_ref.shape[1] // 2
    loads = second_ref.shape[1]
    partial_ref[...] = dot(far_ref[:, :depth], second_ref[:depth])
    parent_ref[...] = parent_rows(
        place_ref, gathered_ref, outer_ref, solved_ref, place_ref[0] & 1, loads
    )


def field_kernel(
    chunk,
    place_ref,
    gathered_ref,
    outer_ref,
    solved_ref,
    swapped_ref,
    first_ref,
    second_ref,
    near_ref,
    far_ref,
    near_part_ref,
    far_part_ref,
    ready_ref,
    field_ref,
    parent_ref,
    pressure,
    finished,
    parent,
    left,
):
    mine = place_ref[0] & 1
    outer, loads = first_ref.shape
    cells, points = near_ref.shape
    depth = points // 2
    cuts = [slice(start, start + chunk) for start in range(0, cells, chunk)]
    copy = pltpu.make_async_copy(ready_ref, parent_ref.at[mine], left.at[0])
    copy.start()
    writes = [copy]
    turns = (
        (mine, solved_ref, first_ref, near_ref, near_part_ref),
        (1 - mine, swapped_ref, second_ref, far_ref, far_part_ref),
    )
    for turn, (box, edge_ref, data_ref, operator_ref, part_ref) in enumerate(turns):
        pressure[turn, : outer - depth] = data_ref[depth:]
        pressure[turn, outer - depth :] = edge_ref[:, :loads]
        for cut in cuts:
            total = part_ref[cut] + dot(operator_ref[cut, depth:], pressure[turn])
            finished[turn, cut] = total.astype(BF16)
            copy = pltpu.make_async_copy(
                finished.at[turn, cut], field_ref.at[box, cut], left.at[len(writes)]
            )
            copy.start()
            writes.append(copy)
    parent[...] = parent_rows(place_ref, gathered_ref, outer_ref, swapped_ref, 1 - mine, loads)
    copy = pltpu.make_async_copy(parent, parent_ref.at[1 - mine], left.at[len(writes)])
    copy.start()
    writes.append(copy)
    finish_copies(writes)


def per_device(dtn_map, boundary_data, solution_op):
    boxes, _, local, points = dtn_map.shape
    edge = boundary_data.shape[2]
    loads = boundary_data.shape[3]
    cells = solution_op.shape[1]
    outer = 3 * edge
    side = lax.axis_index("box") & 1
    core = lax.axis_index("row") & 1
    place = (2 * side + core).astype(jnp.int32).reshape(1)
    whole_map = in_hbm(dtn_map)
    data = in_hbm(boundary_data.reshape(boxes, outer, loads))
    operator = in_hbm(solution_op)
    half = jax.ShapeDtypeStruct((outer, loads), BF16)
    part = pltpu.VMEM((cells, loads), F32)
    own_rows, first = pl.pallas_call(
        start_kernel,
        out_shape=(jax.ShapeDtypeStruct((boxes, local, points), F32), half),
        in_specs=[SMEM_SPEC, HBM_SPEC, HBM_SPEC],
        out_specs=(VMEM_SPEC, VMEM_SPEC),
        scratch_shapes=[pltpu.SemaphoreType.DMA((2,))],
        compiler_params=pltpu.CompilerParams(vmem_limit_bytes=4 << 20),
        name="start",
    )(place, whole_map, data)
    other_rows = exchange(own_rows, "box")
    first, near, near_part = pl.pallas_call(
        early_kernel,
        out_shape=(half, pltpu.VMEM((cells, points), BF16), part),
        in_specs=[SMEM_SPEC, VMEM_SPEC, ANY_SPEC, HBM_SPEC],
        out_specs=(VMEM_SPEC,) * 3,
        scratch_shapes=[pltpu.SemaphoreType.DMA((1,))],
        input_output_aliases={1: 0},
        compiler_params=pltpu.CompilerParams(vmem_limit_bytes=4 << 20),
        cost_estimate=pl.CostEstimate(
            flops=cells * points * loads, bytes_accessed=6 << 20, transcendentals=0
        ),
        name="early",
    )(place, first, own_rows, operator)
    crossed = exchange(first, "box")
    packed = jnp.concatenate(
        [
            own_rows[:, :, outer:] + other_rows[:, :, outer:],
            own_rows[:, :, :outer],
            other_rows[:, :, :outer],
        ],
        axis=2,
    )
    gathered = lax.all_gather(packed, "row", axis=0)
    solved, outer_rows, second, far = pl.pallas_call(
        solve_kernel,
        out_shape=(
            jax.ShapeDtypeStruct((edge, loads + 3 * edge), BF16),
            pltpu.VMEM((boxes, 3, local, points), F32),
            pltpu.VMEM((outer, loads), BF16),
            pltpu.VMEM((cells, points), BF16),
        ),
        in_specs=[SMEM_SPEC] + [VMEM_SPEC] * 3 + [HBM_SPEC] * 3,
        out_specs=(VMEM_SPEC,) * 4,
        scratch_shapes=[
            pltpu.VMEM((edge, edge), F32),
            pltpu.VMEM((edge, edge), F32),
            pltpu.SemaphoreType.DMA((3,)),
        ],
        compiler_params=pltpu.CompilerParams(vmem_limit_bytes=12 << 20),
        name="solve",
    )(place, gathered, first, crossed, whole_map, data, operator)
    swapped = exchange(solved, "row")
    far_part, ready = pl.pallas_call(
        middle_kernel,
        out_shape=(part, pltpu.VMEM((3, local, 2 * outer), F32)),
        in_specs=[SMEM_SPEC] + [VMEM_SPEC] * 5,
        out_specs=(VMEM_SPEC,) * 2,
        compiler_params=pltpu.CompilerParams(vmem_limit_bytes=6 << 20),
        cost_estimate=pl.CostEstimate(
            flops=cells * points * loads, bytes_accessed=6 << 20, transcendentals=0
        ),
        name="middle",
    )(place, gathered, outer_rows, solved, second, far)
    chunk = 256
    interior_field, parent_map = pl.pallas_call(
        functools.partial(field_kernel, chunk),
        out_shape=(
            jax.ShapeDtypeStruct((boxes, cells, loads), BF16),
            jax.ShapeDtypeStruct((boxes, 3, local, 2 * outer), F32),
        ),
        in_specs=[SMEM_SPEC] + [VMEM_SPEC] * 11,
        out_specs=(ANY_SPEC, ANY_SPEC),
        scratch_shapes=[
            pltpu.VMEM((boxes, points - points // 2, loads), BF16),
            pltpu.VMEM((boxes, cells, loads), BF16),
            pltpu.VMEM((3, local, 2 * outer), F32),
            pltpu.SemaphoreType.DMA((boxes * cells // chunk + 2,)),
        ],
        compiler_params=pltpu.CompilerParams(vmem_limit_bytes=16 << 20),
        name="field",
    )(
        place,
        gathered,
        outer_rows,
        solved,
        swapped,
        first,
        second,
        near,
        far,
        near_part,
        far_part,
        ready,
    )
    return (parent_map, interior_field)


def solution(mesh):
    in_specs = (P("box", None, "row", None), P("box", None, None, None), P("box", "row", None))
    out_specs = (P("box", None, "row", None), P("box", "row", None))
    return jax.shard_map(
        per_device, mesh=mesh, in_specs=in_specs, out_specs=out_specs, check_vma=False
    )
```

```python
import functools

import jax
import jax.numpy as jnp
from jax import lax
from jax.experimental import pallas as pl
from jax.experimental.pallas import tpu as pltpu
from jax.sharding import PartitionSpec as P

F32 = jnp.float32
BF16 = jnp.bfloat16
REMAINDER = 2.0**-27
SURE_DOUBLINGS = 4
MOST_DOUBLINGS = 40

SMEM_SPEC = pl.BlockSpec(memory_space=pltpu.SMEM)
VMEM_SPEC = pl.BlockSpec(memory_space=pltpu.VMEM)
HBM_SPEC = pl.BlockSpec(memory_space=pltpu.HBM)
ANY_SPEC = pl.BlockSpec(memory_space=pl.ANY)


def exchange(value, axis):
    pairs = [(source, source ^ 1) for source in range(lax.axis_size(axis))]
    return lax.ppermute(value, axis, pairs)


def in_hbm(value):
    return pltpu.with_memory_space_constraint(value, pltpu.HBM)


def dot(left, right, precision=None):
    return jnp.dot(left, right, precision=precision, preferred_element_type=F32)


def split(value, count):
    pieces = []
    for _ in range(count):
        piece = value.astype(BF16)
        pieces.append(piece)
        value = value - piece.astype(F32)
    return pieces


def split_dot(left, right):
    high, low = split(left, 2)
    right_high, right_low = split(right, 2)
    both = dot(jnp.concatenate([high, low], axis=0), right_high)
    rows = left.shape[0]
    return both[:rows] + (both[rows:] + dot(high, right_low))


def full_dot(left, right):
    return dot(left, right, lax.Precision.HIGHEST)


def start_copies(copies):
    for copy in copies:
        copy.start()


def finish_copies(copies):
    for copy in copies:
        copy.wait()


def start_kernel(place_ref, map_ref, data_ref, rows_ref, first_ref, arrived):
    copies = (
        pltpu.make_async_copy(map_ref.at[:, 3], rows_ref, arrived.at[0]),
        pltpu.make_async_copy(data_ref.at[place_ref[0] & 1], first_ref, arrived.at[1]),
    )
    start_copies(copies)
    finish_copies(copies)


def order_kernel(first_ref, rows_ref, same_ref):
    pass


def early_kernel(
    place_ref,
    first_ref,
    map_ref,
    data_ref,
    operator_ref,
    near_ref,
    partial_ref,
    outer_ref,
    second_ref,
    far_ref,
    arrived,
):
    mine = place_ref[0] & 1
    depth = operator_ref.shape[2] // 2
    copies = (
        pltpu.make_async_copy(operator_ref.at[mine], near_ref, arrived.at[0]),
        pltpu.make_async_copy(operator_ref.at[1 - mine], far_ref, arrived.at[1]),
        pltpu.make_async_copy(data_ref.at[1 - mine], second_ref, arrived.at[2]),
        pltpu.make_async_copy(map_ref.at[:, pl.ds(0, 3)], outer_ref, arrived.at[3]),
    )
    start_copies(copies)
    copies[0].wait()
    partial_ref[...] = dot(near_ref[:, :depth], first_ref[:depth])
    finish_copies(copies[1:])


def solve_kernel(
    place_ref,
    gathered_ref,
    own_ref,
    other_ref,
    solved_ref,
    sums,
    power_ref,
    terms_ref,
):
    mine = place_ref[0] & 1
    edge = sums.shape[0]
    outer, loads = own_ref.shape
    shared = gathered_ref[:, mine, :, :edge].reshape(edge, edge)
    row = lax.broadcasted_iota(jnp.int32, (edge, edge), 0)
    column = lax.broadcasted_iota(jnp.int32, (edge, edge), 1)
    diagonal = row == column
    kept = jnp.where(diagonal, shared, 0.0)
    scale = 1.0 / jnp.sum(kept, axis=1, keepdims=True)
    right_scale = 1.0 / jnp.sum(kept, axis=0, keepdims=True)
    power = jnp.where(diagonal, 0.0, -shared) * scale
    size = jnp.sum(jnp.abs(power), axis=1, keepdims=True)
    norm = jnp.max(size, axis=0, keepdims=True)[0, 0]

    coupling = gathered_ref[:, mine, :, edge:].reshape(edge, 2 * outer)
    parts = dot(jnp.concatenate(split(coupling[:, :outer], 2), axis=0), own_ref[...])
    parts += dot(jnp.concatenate(split(coupling[:, outer:], 2), axis=0), other_ref[...])
    terms = parts[:edge] + parts[edge:]

    total = jnp.where(diagonal, 1.0, power)
    power = split_dot(power, power)
    for _ in range(SURE_DOUBLINGS - 1):
        both = split_dot(jnp.concatenate([total, power], axis=0), power)
        total = total + both[:edge]
        power = both[edge:]
    total = total + split_dot(total, power)
    sums[...] = total
    power_ref[...] = power
    terms_ref[...] = terms

    def hand_out(total, terms):
        inverse = total * right_scale
        solved_ref[:, :loads] = (-split_dot(inverse, terms)).astype(BF16)
        for order, piece in enumerate(split(inverse, 3)):
            solved_ref[:, loads + order * edge : loads + (order + 1) * edge] = piece

    hand_out(total, terms)
    bound = norm
    for _ in range(SURE_DOUBLINGS + 1):
        bound = bound * bound

    @pl.when(bound > REMAINDER)
    def _():
        last = power_ref[...]
        power_ref[...] = full_dot(last, last)

        def more(carry):
            left, count = carry
            return jnp.logical_and(left > REMAINDER, count < MOST_DOUBLINGS)

        def double(carry):
            left, count = carry
            held = power_ref[...]
            both = full_dot(jnp.concatenate([sums[...], held], axis=0), held)
            sums[...] = sums[...] + both[:edge]
            power_ref[...] = both[edge:]
            return left * left, count + 1

        lax.while_loop(more, double, (bound, jnp.int32(0)))
        hand_out(sums[...], terms_ref[...])


def parent_rows(place_ref, gathered_ref, outer_ref, solved_ref, box, loads):
    edge = solved_ref.shape[0]
    outer = 3 * edge
    inverse = jnp.zeros((edge, edge), F32)
    for order in (2, 1, 0):
        inverse = inverse + solved_ref[:, loads + order * edge : loads + (order + 1) * edge].astype(F32)
    rows = outer_ref[box].reshape(-1, 4 * edge)
    weights = split_dot(rows[:, outer:], inverse)
    coupling = gathered_ref[:, box, :, edge:].reshape(edge, 2 * outer)
    change = split_dot(weights, coupling)
    own = rows[:, :outer] - change[:, :outer]
    other = -change[:, outer:]
    is_alpha = place_ref[0] < 2
    left = jnp.where(is_alpha, own, other)
    right = jnp.where(is_alpha, other, own)
    return jnp.concatenate([left, right], axis=1).reshape(3, -1, 2 * outer)


def middle_kernel(
    place_ref, gathered_ref, outer_ref, solved_ref, second_ref, far_ref, partial_ref, parent_ref
):
    depth = far_ref.shape[1] // 2
    loads = second_ref.shape[1]
    partial_ref[...] = dot(far_ref[:, :depth], second_ref[:depth])
    parent_ref[...] = parent_rows(
        place_ref, gathered_ref, outer_ref, solved_ref, place_ref[0] & 1, loads
    )


def field_kernel(
    chunk,
    place_ref,
    gathered_ref,
    outer_ref,
    solved_ref,
    swapped_ref,
    first_ref,
    second_ref,
    near_ref,
    far_ref,
    near_part_ref,
    far_part_ref,
    ready_ref,
    field_ref,
    parent_ref,
    pressure,
    finished,
    parent,
    left,
):
    mine = place_ref[0] & 1
    outer, loads = first_ref.shape
    cells, points = near_ref.shape
    depth = points // 2
    cuts = [slice(start, start + chunk) for start in range(0, cells, chunk)]
    copy = pltpu.make_async_copy(ready_ref, parent_ref.at[mine], left.at[0])
    copy.start()
    writes = [copy]
    turns = (
        (mine, solved_ref, first_ref, near_ref, near_part_ref),
        (1 - mine, swapped_ref, second_ref, far_ref, far_part_ref),
    )
    for turn, (box, edge_ref, data_ref, operator_ref, part_ref) in enumerate(turns):
        pressure[turn, : outer - depth] = data_ref[depth:]
        pressure[turn, outer - depth :] = edge_ref[:, :loads]
        for cut in cuts:
            total = part_ref[cut] + dot(operator_ref[cut, depth:], pressure[turn])
            finished[turn, cut] = total.astype(BF16)
            copy = pltpu.make_async_copy(
                finished.at[turn, cut], field_ref.at[box, cut], left.at[len(writes)]
            )
            copy.start()
            writes.append(copy)
    parent[...] = parent_rows(place_ref, gathered_ref, outer_ref, swapped_ref, 1 - mine, loads)
    copy = pltpu.make_async_copy(parent, parent_ref.at[1 - mine], left.at[len(writes)])
    copy.start()
    writes.append(copy)
    finish_copies(writes)


def per_device(dtn_map, boundary_data, solution_op):
    boxes, _, local, points = dtn_map.shape
    edge = boundary_data.shape[2]
    loads = boundary_data.shape[3]
    cells = solution_op.shape[1]
    outer = 3 * edge
    side = lax.axis_index("box") & 1
    core = lax.axis_index("row") & 1
    place = (2 * side + core).astype(jnp.int32).reshape(1)
    whole_map = in_hbm(dtn_map)
    data = in_hbm(boundary_data.reshape(boxes, outer, loads))
    operator = in_hbm(solution_op)
    half = jax.ShapeDtypeStruct((outer, loads), BF16)
    part = pltpu.VMEM((cells, loads), F32)
    own_rows, first = pl.pallas_call(
        start_kernel,
        out_shape=(jax.ShapeDtypeStruct((boxes, local, points), F32), half),
        in_specs=[SMEM_SPEC, HBM_SPEC, HBM_SPEC],
        out_specs=(VMEM_SPEC, VMEM_SPEC),
        scratch_shapes=[pltpu.SemaphoreType.DMA((2,))],
        compiler_params=pltpu.CompilerParams(vmem_limit_bytes=4 << 20),
        name="start",
    )(place, whole_map, data)
    other_rows = exchange(own_rows, "box")
    first = pl.pallas_call(
        order_kernel,
        out_shape=half,
        in_specs=[ANY_SPEC, ANY_SPEC],
        out_specs=ANY_SPEC,
        input_output_aliases={0: 0},
        compiler_params=pltpu.CompilerParams(vmem_limit_bytes=1 << 20),
        name="order",
    )(first, own_rows)
    crossed = exchange(first, "box")
    near, near_part, outer_rows, second, far = pl.pallas_call(
        early_kernel,
        out_shape=(
            pltpu.VMEM((cells, points), BF16),
            part,
            pltpu.VMEM((boxes, 3, local, points), F32),
            pltpu.VMEM((outer, loads), BF16),
            pltpu.VMEM((cells, points), BF16),
        ),
        in_specs=[SMEM_SPEC, VMEM_SPEC, HBM_SPEC, HBM_SPEC, HBM_SPEC],
        out_specs=(VMEM_SPEC,) * 5,
        scratch_shapes=[pltpu.SemaphoreType.DMA((4,))],
        compiler_params=pltpu.CompilerParams(vmem_limit_bytes=4 << 20),
        cost_estimate=pl.CostEstimate(
            flops=cells * points * loads, bytes_accessed=6 << 20, transcendentals=0
        ),
        name="early",
    )(place, first, whole_map, data, operator)
    other_rows, near = lax.optimization_barrier((other_rows, near))
    packed = jnp.concatenate(
        [
            own_rows[:, :, outer:] + other_rows[:, :, outer:],
            own_rows[:, :, :outer],
            other_rows[:, :, :outer],
        ],
        axis=2,
    )
    gathered = lax.all_gather(packed, "row", axis=0)
    solved = pl.pallas_call(
        solve_kernel,
        out_shape=jax.ShapeDtypeStruct((edge, loads + 3 * edge), BF16),
        in_specs=[SMEM_SPEC] + [VMEM_SPEC] * 3,
        out_specs=VMEM_SPEC,
        scratch_shapes=[
            pltpu.VMEM((edge, edge), F32),
            pltpu.VMEM((edge, edge), F32),
            pltpu.VMEM((edge, loads), F32),
        ],
        compiler_params=pltpu.CompilerParams(vmem_limit_bytes=12 << 20),
        name="solve",
    )(place, gathered, first, crossed)
    swapped = exchange(solved, "row")
    far_part, ready = pl.pallas_call(
        middle_kernel,
        out_shape=(part, pltpu.VMEM((3, local, 2 * outer), F32)),
        in_specs=[SMEM_SPEC] + [VMEM_SPEC] * 5,
        out_specs=(VMEM_SPEC,) * 2,
        compiler_params=pltpu.CompilerParams(vmem_limit_bytes=6 << 20),
        cost_estimate=pl.CostEstimate(
            flops=cells * points * loads, bytes_accessed=6 << 20, transcendentals=0
        ),
        name="middle",
    )(place, gathered, outer_rows, solved, second, far)
    chunk = 256
    interior_field, parent_map = pl.pallas_call(
        functools.partial(field_kernel, chunk),
        out_shape=(
            jax.ShapeDtypeStruct((boxes, cells, loads), BF16),
            jax.ShapeDtypeStruct((boxes, 3, local, 2 * outer), F32),
        ),
        in_specs=[SMEM_SPEC] + [VMEM_SPEC] * 11,
        out_specs=(ANY_SPEC, ANY_SPEC),
        scratch_shapes=[
            pltpu.VMEM((boxes, points - points // 2, loads), BF16),
            pltpu.VMEM((boxes, cells, loads), BF16),
            pltpu.VMEM((3, local, 2 * outer), F32),
            pltpu.SemaphoreType.DMA((boxes * cells // chunk + 2,)),
        ],
        compiler_params=pltpu.CompilerParams(vmem_limit_bytes=16 << 20),
        name="field",
    )(
        place,
        gathered,
        outer_rows,
        solved,
        swapped,
        first,
        second,
        near,
        far,
        near_part,
        far_part,
        ready,
    )
    return (parent_map, interior_field)


def solution(mesh):
    in_specs = (P("box", None, "row", None), P("box", None, None, None), P("box", "row", None))
    out_specs = (P("box", None, "row", None), P("box", "row", None))
    return jax.shard_map(
        per_device, mesh=mesh, in_specs=in_specs, out_specs=out_specs, check_vma=False
    )
```

```python
import jax
import jax.numpy as jnp
from jax import lax
from jax.experimental import pallas as pl
from jax.experimental.pallas import tpu as pltpu
from jax.sharding import PartitionSpec as P

F32 = jnp.float32
BF16 = jnp.bfloat16
REMAINDER = 2.0**-27
SURE_DOUBLINGS = 4
MOST_DOUBLINGS = 40

SMEM_SPEC = pl.BlockSpec(memory_space=pltpu.SMEM)
VMEM_SPEC = pl.BlockSpec(memory_space=pltpu.VMEM)
HBM_SPEC = pl.BlockSpec(memory_space=pltpu.HBM)
ANY_SPEC = pl.BlockSpec(memory_space=pl.ANY)


def exchange(value, axis):
    pairs = [(source, source ^ 1) for source in range(lax.axis_size(axis))]
    return lax.ppermute(value, axis, pairs)


def in_hbm(value):
    return pltpu.with_memory_space_constraint(value, pltpu.HBM)


def dot(left, right, precision=None):
    return jnp.dot(left, right, precision=precision, preferred_element_type=F32)


def split(value, count):
    pieces = []
    for _ in range(count):
        piece = value.astype(BF16)
        pieces.append(piece)
        value = value - piece.astype(F32)
    return pieces


def split_dot(left, right):
    high, low = split(left, 2)
    right_high, right_low = split(right, 2)
    both = dot(jnp.concatenate([high, low], axis=0), right_high)
    rows = left.shape[0]
    return both[:rows] + (both[rows:] + dot(high, right_low))


def full_dot(left, right):
    return dot(left, right, lax.Precision.HIGHEST)


def start_copies(copies):
    for copy in copies:
        copy.start()


def finish_copies(copies):
    for copy in copies:
        copy.wait()


def start_kernel(map_ref, rows_ref, arrived):
    copy = pltpu.make_async_copy(map_ref.at[:, 3], rows_ref, arrived.at[0])
    copy.start()
    copy.wait()


def early_kernel(
    place_ref,
    rows_ref,
    map_ref,
    data_ref,
    operator_ref,
    first_ref,
    near_ref,
    partial_ref,
    outer_ref,
    second_ref,
    far_ref,
    arrived,
):
    mine = place_ref[0] & 1
    depth = operator_ref.shape[2] // 2
    copies = (
        pltpu.make_async_copy(data_ref.at[mine], first_ref, arrived.at[0]),
        pltpu.make_async_copy(operator_ref.at[mine], near_ref, arrived.at[1]),
        pltpu.make_async_copy(operator_ref.at[1 - mine], far_ref, arrived.at[2]),
        pltpu.make_async_copy(data_ref.at[1 - mine], second_ref, arrived.at[3]),
        pltpu.make_async_copy(map_ref.at[:, pl.ds(0, 3)], outer_ref, arrived.at[4]),
    )
    start_copies(copies)
    finish_copies(copies[:2])
    partial_ref[...] = dot(near_ref[:, :depth], first_ref[:depth])
    finish_copies(copies[2:])


def solve_kernel(
    place_ref,
    gathered_ref,
    own_ref,
    other_ref,
    solved_ref,
    sums,
    power_ref,
    terms_ref,
):
    mine = place_ref[0] & 1
    edge = sums.shape[0]
    outer, loads = own_ref.shape
    shared = gathered_ref[:, mine, :, :edge].reshape(edge, edge)
    row = lax.broadcasted_iota(jnp.int32, (edge, edge), 0)
    column = lax.broadcasted_iota(jnp.int32, (edge, edge), 1)
    diagonal = row == column
    kept = jnp.where(diagonal, shared, 0.0)
    scale = 1.0 / jnp.sum(kept, axis=1, keepdims=True)
    right_scale = 1.0 / jnp.sum(kept, axis=0, keepdims=True)
    power = jnp.where(diagonal, 0.0, -shared) * scale
    size = jnp.sum(jnp.abs(power), axis=1, keepdims=True)
    norm = jnp.max(size, axis=0, keepdims=True)[0, 0]

    coupling = gathered_ref[:, mine, :, edge:].reshape(edge, 2 * outer)
    parts = dot(jnp.concatenate(split(coupling[:, :outer], 2), axis=0), own_ref[...])
    parts += dot(jnp.concatenate(split(coupling[:, outer:], 2), axis=0), other_ref[...])
    terms = parts[:edge] + parts[edge:]

    total = jnp.where(diagonal, 1.0, power)
    power = split_dot(power, power)
    for _ in range(SURE_DOUBLINGS - 1):
        both = split_dot(jnp.concatenate([total, power], axis=0), power)
        total = total + both[:edge]
        power = both[edge:]
    total = total + split_dot(total, power)
    sums[...] = total
    power_ref[...] = power
    terms_ref[...] = terms

    def hand_out(total, terms):
        inverse = total * right_scale
        solved_ref[:, :loads] = (-split_dot(inverse, terms)).astype(BF16)
        for order, piece in enumerate(split(inverse, 3)):
            solved_ref[:, loads + order * edge : loads + (order + 1) * edge] = piece

    hand_out(total, terms)
    bound = norm
    for _ in range(SURE_DOUBLINGS + 1):
        bound = bound * bound

    @pl.when(bound > REMAINDER)
    def _():
        last = power_ref[...]
        power_ref[...] = full_dot(last, last)

        def more(carry):
            left, count = carry
            return jnp.logical_and(left > REMAINDER, count < MOST_DOUBLINGS)

        def double(carry):
            left, count = carry
            held = power_ref[...]
            both = full_dot(jnp.concatenate([sums[...], held], axis=0), held)
            sums[...] = sums[...] + both[:edge]
            power_ref[...] = both[edge:]
            return left * left, count + 1

        lax.while_loop(more, double, (bound, jnp.int32(0)))
        hand_out(sums[...], terms_ref[...])


def parent_rows(place_ref, gathered_ref, outer_ref, solved_ref, box, loads):
    edge = solved_ref.shape[0]
    outer = 3 * edge
    inverse = jnp.zeros((edge, edge), F32)
    for order in (2, 1, 0):
        inverse = inverse + solved_ref[:, loads + order * edge : loads + (order + 1) * edge].astype(F32)
    rows = outer_ref[box].reshape(-1, 4 * edge)
    weights = split_dot(rows[:, outer:], inverse)
    coupling = gathered_ref[:, box, :, edge:].reshape(edge, 2 * outer)
    change = split_dot(weights, coupling)
    own = rows[:, :outer] - change[:, :outer]
    other = -change[:, outer:]
    is_alpha = place_ref[0] < 2
    left = jnp.where(is_alpha, own, other)
    right = jnp.where(is_alpha, other, own)
    return jnp.concatenate([left, right], axis=1).reshape(3, -1, 2 * outer)


def finish_field(box, edge_ref, data_ref, operator_ref, part_ref, field_ref, pressure, finished, left):
    outer = data_ref.shape[0]
    cells, points = operator_ref.shape
    depth = points // 2
    loads = data_ref.shape[1]
    pieces = left.shape[0] - 1
    chunk = cells // pieces
    pressure[: outer - depth] = data_ref[depth:]
    pressure[outer - depth :] = edge_ref[:, :loads]
    writes = []
    for order in range(pieces):
        cut = slice(order * chunk, (order + 1) * chunk)
        total = part_ref[cut] + dot(operator_ref[cut, depth:], pressure[...])
        finished[cut] = total.astype(BF16)
        copy = pltpu.make_async_copy(finished.at[cut], field_ref.at[box, cut], left.at[order])
        copy.start()
        writes.append(copy)
    return writes


def finish_parent(place_ref, gathered_ref, outer_ref, edge_ref, box, loads, parent_ref, parent, left):
    parent[...] = parent_rows(place_ref, gathered_ref, outer_ref, edge_ref, box, loads)
    copy = pltpu.make_async_copy(parent, parent_ref.at[box], left.at[left.shape[0] - 1])
    copy.start()
    return [copy]


def middle_kernel(
    place_ref,
    gathered_ref,
    outer_ref,
    solved_ref,
    first_ref,
    second_ref,
    near_ref,
    far_ref,
    near_part_ref,
    far_part_ref,
    field_ref,
    parent_ref,
    pressure,
    finished,
    parent,
    left,
):
    mine = place_ref[0] & 1
    loads = first_ref.shape[1]
    depth = far_ref.shape[1] // 2
    writes = finish_field(
        mine, solved_ref, first_ref, near_ref, near_part_ref, field_ref, pressure, finished, left
    )
    writes += finish_parent(
        place_ref, gathered_ref, outer_ref, solved_ref, mine, loads, parent_ref, parent, left
    )
    far_part_ref[...] = dot(far_ref[:, :depth], second_ref[:depth])
    finish_copies(writes)


def field_kernel(
    place_ref,
    gathered_ref,
    outer_ref,
    swapped_ref,
    second_ref,
    far_ref,
    far_part_ref,
    made_field_ref,
    made_parent_ref,
    field_ref,
    parent_ref,
    pressure,
    finished,
    parent,
    left,
):
    other = 1 - (place_ref[0] & 1)
    loads = second_ref.shape[1]
    writes = finish_field(
        other, swapped_ref, second_ref, far_ref, far_part_ref, field_ref, pressure, finished, left
    )
    writes += finish_parent(
        place_ref, gathered_ref, outer_ref, swapped_ref, other, loads, parent_ref, parent, left
    )
    finish_copies(writes)


def per_device(dtn_map, boundary_data, solution_op):
    boxes, _, local, points = dtn_map.shape
    edge = boundary_data.shape[2]
    loads = boundary_data.shape[3]
    cells = solution_op.shape[1]
    outer = 3 * edge
    side = lax.axis_index("box") & 1
    core = lax.axis_index("row") & 1
    place = (2 * side + core).astype(jnp.int32).reshape(1)
    whole_map = in_hbm(dtn_map)
    data = in_hbm(boundary_data.reshape(boxes, outer, loads))
    operator = in_hbm(solution_op)
    half = jax.ShapeDtypeStruct((outer, loads), BF16)
    part = pltpu.VMEM((cells, loads), F32)
    own_rows = pl.pallas_call(
        start_kernel,
        out_shape=jax.ShapeDtypeStruct((boxes, local, points), F32),
        in_specs=[HBM_SPEC],
        out_specs=VMEM_SPEC,
        scratch_shapes=[pltpu.SemaphoreType.DMA((1,))],
        compiler_params=pltpu.CompilerParams(vmem_limit_bytes=4 << 20),
        name="start",
    )(whole_map)
    other_rows = exchange(own_rows, "box")
    first, near, near_part, outer_rows, second, far = pl.pallas_call(
        early_kernel,
        out_shape=(
            half,
            pltpu.VMEM((cells, points), BF16),
            part,
            pltpu.VMEM((boxes, 3, local, points), F32),
            pltpu.VMEM((outer, loads), BF16),
            pltpu.VMEM((cells, points), BF16),
        ),
        in_specs=[SMEM_SPEC, ANY_SPEC, HBM_SPEC, HBM_SPEC, HBM_SPEC],
        out_specs=(VMEM_SPEC,) * 6,
        scratch_shapes=[pltpu.SemaphoreType.DMA((5,))],
        compiler_params=pltpu.CompilerParams(vmem_limit_bytes=4 << 20),
        cost_estimate=pl.CostEstimate(
            flops=cells * points * loads, bytes_accessed=6 << 20, transcendentals=0
        ),
        name="early",
    )(place, own_rows, whole_map, data, operator)
    crossed = exchange(first, "box")
    other_rows, near = lax.optimization_barrier((other_rows, near))
    packed = jnp.concatenate(
        [
            own_rows[:, :, outer:] + other_rows[:, :, outer:],
            own_rows[:, :, :outer],
            other_rows[:, :, :outer],
        ],
        axis=2,
    )
    gathered = lax.all_gather(packed, "row", axis=0)
    solved = pl.pallas_call(
        solve_kernel,
        out_shape=jax.ShapeDtypeStruct((edge, loads + 3 * edge), BF16),
        in_specs=[SMEM_SPEC] + [VMEM_SPEC] * 3,
        out_specs=VMEM_SPEC,
        scratch_shapes=[
            pltpu.VMEM((edge, edge), F32),
            pltpu.VMEM((edge, edge), F32),
            pltpu.VMEM((edge, loads), F32),
        ],
        compiler_params=pltpu.CompilerParams(vmem_limit_bytes=12 << 20),
        name="solve",
    )(place, gathered, first, crossed)
    swapped = exchange(solved, "row")
    outputs = (
        jax.ShapeDtypeStruct((boxes, cells, loads), BF16),
        jax.ShapeDtypeStruct((boxes, 3, local, 2 * outer), F32),
    )

    def scratch(pieces):
        return [
            pltpu.VMEM((points - points // 2, loads), BF16),
            pltpu.VMEM((cells, loads), BF16),
            pltpu.VMEM((3, local, 2 * outer), F32),
            pltpu.SemaphoreType.DMA((pieces + 1,)),
        ]

    far_part, *made = pl.pallas_call(
        middle_kernel,
        out_shape=(part,) + outputs,
        in_specs=[SMEM_SPEC] + [VMEM_SPEC] * 8,
        out_specs=(VMEM_SPEC, ANY_SPEC, ANY_SPEC),
        scratch_shapes=scratch(8),
        compiler_params=pltpu.CompilerParams(vmem_limit_bytes=10 << 20),
        cost_estimate=pl.CostEstimate(
            flops=2 * cells * points * loads, bytes_accessed=6 << 20, transcendentals=0
        ),
        name="middle",
    )(place, gathered, outer_rows, solved, first, second, near, far, near_part)
    interior_field, parent_map = pl.pallas_call(
        field_kernel,
        out_shape=outputs,
        in_specs=[SMEM_SPEC] + [VMEM_SPEC] * 6 + [ANY_SPEC] * 2,
        out_specs=(ANY_SPEC, ANY_SPEC),
        scratch_shapes=scratch(8),
        input_output_aliases={7: 0, 8: 1},
        compiler_params=pltpu.CompilerParams(vmem_limit_bytes=10 << 20),
        name="field",
    )(place, gathered, outer_rows, swapped, second, far, far_part, *made)
    return (parent_map, interior_field)


def solution(mesh):
    in_specs = (P("box", None, "row", None), P("box", None, None, None), P("box", "row", None))
    out_specs = (P("box", None, "row", None), P("box", "row", None))
    return jax.shard_map(
        per_device, mesh=mesh, in_specs=in_specs, out_specs=out_specs, check_vma=False
    )
```

```python
import jax
import jax.numpy as jnp
from jax import lax
from jax.experimental import pallas as pl
from jax.experimental.pallas import tpu as pltpu
from jax.sharding import PartitionSpec as P

F32 = jnp.float32
BF16 = jnp.bfloat16
REMAINDER = 2.0**-27
SURE_DOUBLINGS = 4
MOST_DOUBLINGS = 40

SMEM_SPEC = pl.BlockSpec(memory_space=pltpu.SMEM)
VMEM_SPEC = pl.BlockSpec(memory_space=pltpu.VMEM)
HBM_SPEC = pl.BlockSpec(memory_space=pltpu.HBM)
ANY_SPEC = pl.BlockSpec(memory_space=pl.ANY)


def exchange(value, axis):
    pairs = [(source, source ^ 1) for source in range(lax.axis_size(axis))]
    return lax.ppermute(value, axis, pairs)


def in_hbm(value):
    return pltpu.with_memory_space_constraint(value, pltpu.HBM)


def dot(left, right, precision=None):
    return jnp.dot(left, right, precision=precision, preferred_element_type=F32)


def split(value, count):
    pieces = []
    for _ in range(count):
        piece = value.astype(BF16)
        pieces.append(piece)
        value = value - piece.astype(F32)
    return pieces


def split_dot(left, right):
    high, low = split(left, 2)
    right_high, right_low = split(right, 2)
    both = dot(jnp.concatenate([high, low], axis=0), right_high)
    rows = left.shape[0]
    return both[:rows] + (both[rows:] + dot(high, right_low))


def full_dot(left, right):
    return dot(left, right, lax.Precision.HIGHEST)


def start_copies(copies):
    for copy in copies:
        copy.start()


def finish_copies(copies):
    for copy in copies:
        copy.wait()


def start_kernel(map_ref, rows_ref, arrived):
    copy = pltpu.make_async_copy(map_ref.at[:, 3], rows_ref, arrived.at[0])
    copy.start()
    copy.wait()


def bring_operators(
    mine, map_ref, data_ref, operator_ref, near_ref, partial_ref, outer_ref, second_ref, far_ref, arrived
):
    copies = (
        pltpu.make_async_copy(operator_ref.at[mine], near_ref, arrived.at[1]),
        pltpu.make_async_copy(operator_ref.at[1 - mine], far_ref, arrived.at[2]),
        pltpu.make_async_copy(data_ref.at[1 - mine], second_ref, arrived.at[3]),
        pltpu.make_async_copy(map_ref.at[:, pl.ds(0, 3)], outer_ref, arrived.at[4]),
    )
    start_copies(copies)

    def finish(first_ref):
        depth = operator_ref.shape[2] // 2
        copies[0].wait()
        partial_ref[...] = dot(near_ref[:, :depth], first_ref[:depth])
        finish_copies(copies[1:])

    return finish


def early_kernel(
    place_ref, rows_ref, map_ref, data_ref, operator_ref, first_ref, *refs
):
    mine = place_ref[0] & 1
    arrived = refs[-1]
    postponed = place_ref[0] >= 4
    copy = pltpu.make_async_copy(data_ref.at[mine], first_ref, arrived.at[0])

    @pl.when(postponed)
    def _():
        copy.start()
        copy.wait()

    @pl.when(jnp.logical_not(postponed))
    def _():
        copy.start()
        finish = bring_operators(mine, map_ref, data_ref, operator_ref, *refs)
        copy.wait()
        finish(first_ref)


def late_kernel(place_ref, solved_ref, map_ref, data_ref, operator_ref, first_ref, *refs):
    @pl.when(place_ref[0] >= 4)
    def _():
        finish = bring_operators(
            place_ref[0] & 1, map_ref, data_ref, operator_ref, *refs[5:]
        )
        finish(first_ref)


def solve_kernel(
    place_ref,
    gathered_ref,
    own_ref,
    other_ref,
    solved_ref,
    sums,
    power_ref,
    terms_ref,
):
    mine = place_ref[0] & 1
    edge = sums.shape[0]
    outer, loads = own_ref.shape
    shared = gathered_ref[:, mine, :, :edge].reshape(edge, edge)
    row = lax.broadcasted_iota(jnp.int32, (edge, edge), 0)
    column = lax.broadcasted_iota(jnp.int32, (edge, edge), 1)
    diagonal = row == column
    kept = jnp.where(diagonal, shared, 0.0)
    scale = 1.0 / jnp.sum(kept, axis=1, keepdims=True)
    right_scale = 1.0 / jnp.sum(kept, axis=0, keepdims=True)
    power = jnp.where(diagonal, 0.0, -shared) * scale
    size = jnp.sum(jnp.abs(power), axis=1, keepdims=True)
    norm = jnp.max(size, axis=0, keepdims=True)[0, 0]

    coupling = gathered_ref[:, mine, :, edge:].reshape(edge, 2 * outer)
    pieces = jnp.concatenate(split(coupling, 2), axis=0)
    block = 2 * edge
    mixed = jnp.concatenate([own_ref[block:], other_ref[:edge]], axis=0)
    parts = dot(pieces[:, :block], own_ref[:block])
    parts += dot(pieces[:, block : 2 * block], mixed)
    parts += dot(pieces[:, 2 * block :], other_ref[edge:])
    terms = parts[:edge] + parts[edge:]

    total = jnp.where(diagonal, 1.0, power)
    power = split_dot(power, power)
    for _ in range(SURE_DOUBLINGS - 1):
        both = split_dot(jnp.concatenate([total, power], axis=0), power)
        total = total + both[:edge]
        power = both[edge:]
    total = total + split_dot(total, power)
    sums[...] = total
    power_ref[...] = power
    terms_ref[...] = terms

    def hand_out(total, terms):
        inverse = total * right_scale
        solved_ref[:, :loads] = (-split_dot(inverse, terms)).astype(BF16)
        for order, piece in enumerate(split(inverse, 3)):
            solved_ref[:, loads + order * edge : loads + (order + 1) * edge] = piece

    hand_out(total, terms)
    bound = norm
    for _ in range(SURE_DOUBLINGS + 1):
        bound = bound * bound

    @pl.when(bound > REMAINDER)
    def _():
        last = power_ref[...]
        power_ref[...] = full_dot(last, last)

        def more(carry):
            left, count = carry
            return jnp.logical_and(left > REMAINDER, count < MOST_DOUBLINGS)

        def double(carry):
            left, count = carry
            held = power_ref[...]
            both = full_dot(jnp.concatenate([sums[...], held], axis=0), held)
            sums[...] = sums[...] + both[:edge]
            power_ref[...] = both[edge:]
            return left * left, count + 1

        lax.while_loop(more, double, (bound, jnp.int32(0)))
        hand_out(sums[...], terms_ref[...])


def parent_rows(place_ref, gathered_ref, outer_ref, solved_ref, box, loads):
    edge = solved_ref.shape[0]
    outer = 3 * edge
    inverse = jnp.zeros((edge, edge), F32)
    for order in (2, 1, 0):
        inverse = inverse + solved_ref[:, loads + order * edge : loads + (order + 1) * edge].astype(F32)
    rows = outer_ref[box].reshape(-1, 4 * edge)
    weights = split_dot(rows[:, outer:], inverse)
    coupling = gathered_ref[:, box, :, edge:].reshape(edge, 2 * outer)
    change = split_dot(weights, coupling)
    own = rows[:, :outer] - change[:, :outer]
    other = -change[:, outer:]
    is_alpha = (place_ref[0] & 2) == 0
    left = jnp.where(is_alpha, own, other)
    right = jnp.where(is_alpha, other, own)
    return jnp.concatenate([left, right], axis=1).reshape(3, -1, 2 * outer)


def finish_field(box, edge_ref, data_ref, operator_ref, part_ref, field_ref, pressure, finished, left):
    outer = data_ref.shape[0]
    cells, points = operator_ref.shape
    depth = points // 2
    loads = data_ref.shape[1]
    pieces = left.shape[0] - 1
    chunk = cells // pieces
    pressure[: outer - depth] = data_ref[depth:]
    pressure[outer - depth :] = edge_ref[:, :loads]
    writes = []
    for order in range(pieces):
        cut = slice(order * chunk, (order + 1) * chunk)
        total = part_ref[cut] + dot(operator_ref[cut, depth:], pressure[...])
        finished[cut] = total.astype(BF16)
        copy = pltpu.make_async_copy(finished.at[cut], field_ref.at[box, cut], left.at[order])
        copy.start()
        writes.append(copy)
    return writes


def finish_parent(place_ref, gathered_ref, outer_ref, edge_ref, box, loads, parent_ref, parent, left):
    parent[...] = parent_rows(place_ref, gathered_ref, outer_ref, edge_ref, box, loads)
    copy = pltpu.make_async_copy(parent, parent_ref.at[box], left.at[left.shape[0] - 1])
    copy.start()
    return [copy]


def middle_kernel(
    place_ref,
    gathered_ref,
    outer_ref,
    solved_ref,
    first_ref,
    second_ref,
    near_ref,
    far_ref,
    near_part_ref,
    far_part_ref,
    field_ref,
    parent_ref,
    pressure,
    finished,
    parent,
    left,
):
    mine = place_ref[0] & 1
    loads = first_ref.shape[1]
    depth = far_ref.shape[1] // 2
    writes = finish_field(
        mine, solved_ref, first_ref, near_ref, near_part_ref, field_ref, pressure, finished, left
    )
    writes += finish_parent(
        place_ref, gathered_ref, outer_ref, solved_ref, mine, loads, parent_ref, parent, left
    )
    far_part_ref[...] = dot(far_ref[:, :depth], second_ref[:depth])
    finish_copies(writes)


def field_kernel(
    place_ref,
    gathered_ref,
    outer_ref,
    swapped_ref,
    second_ref,
    far_ref,
    far_part_ref,
    made_field_ref,
    made_parent_ref,
    field_ref,
    parent_ref,
    pressure,
    finished,
    parent,
    left,
):
    other = 1 - (place_ref[0] & 1)
    loads = second_ref.shape[1]
    writes = finish_field(
        other, swapped_ref, second_ref, far_ref, far_part_ref, field_ref, pressure, finished, left
    )
    writes += finish_parent(
        place_ref, gathered_ref, outer_ref, swapped_ref, other, loads, parent_ref, parent, left
    )
    finish_copies(writes)


def per_device(dtn_map, boundary_data, solution_op):
    boxes, _, local, points = dtn_map.shape
    edge = boundary_data.shape[2]
    loads = boundary_data.shape[3]
    cells = solution_op.shape[1]
    outer = 3 * edge
    side = lax.axis_index("box") & 1
    core = lax.axis_index("row") & 1
    upper = jnp.where(2 * lax.axis_index("row") >= lax.axis_size("row"), 4, 0)
    place = (upper + 2 * side + core).astype(jnp.int32).reshape(1)
    whole_map = in_hbm(dtn_map)
    data = in_hbm(boundary_data.reshape(boxes, outer, loads))
    operator = in_hbm(solution_op)
    half = jax.ShapeDtypeStruct((outer, loads), BF16)
    part = pltpu.VMEM((cells, loads), F32)
    own_rows = pl.pallas_call(
        start_kernel,
        out_shape=jax.ShapeDtypeStruct((boxes, local, points), F32),
        in_specs=[HBM_SPEC],
        out_specs=VMEM_SPEC,
        scratch_shapes=[pltpu.SemaphoreType.DMA((1,))],
        compiler_params=pltpu.CompilerParams(vmem_limit_bytes=4 << 20),
        name="start",
    )(whole_map)
    other_rows = exchange(own_rows, "box")
    brought = (
        pltpu.VMEM((cells, points), BF16),
        part,
        pltpu.VMEM((boxes, 3, local, points), F32),
        pltpu.VMEM((outer, loads), BF16),
        pltpu.VMEM((cells, points), BF16),
    )
    first, near, *others = pl.pallas_call(
        early_kernel,
        out_shape=(half,) + brought,
        in_specs=[SMEM_SPEC, ANY_SPEC, HBM_SPEC, HBM_SPEC, HBM_SPEC],
        out_specs=(VMEM_SPEC,) * 6,
        scratch_shapes=[pltpu.SemaphoreType.DMA((5,))],
        compiler_params=pltpu.CompilerParams(vmem_limit_bytes=4 << 20),
        cost_estimate=pl.CostEstimate(
            flops=cells * points * loads, bytes_accessed=6 << 20, transcendentals=0
        ),
        name="early",
    )(place, own_rows, whole_map, data, operator)
    crossed = exchange(first, "box")
    other_rows, near = lax.optimization_barrier((other_rows, near))
    packed = jnp.concatenate(
        [
            own_rows[:, :, outer:] + other_rows[:, :, outer:],
            own_rows[:, :, :outer],
            other_rows[:, :, :outer],
        ],
        axis=2,
    )
    gathered = lax.all_gather(packed, "row", axis=0)
    solved = pl.pallas_call(
        solve_kernel,
        out_shape=jax.ShapeDtypeStruct((edge, loads + 3 * edge), BF16),
        in_specs=[SMEM_SPEC] + [VMEM_SPEC] * 3,
        out_specs=VMEM_SPEC,
        scratch_shapes=[
            pltpu.VMEM((edge, edge), F32),
            pltpu.VMEM((edge, edge), F32),
            pltpu.VMEM((edge, loads), F32),
        ],
        compiler_params=pltpu.CompilerParams(vmem_limit_bytes=12 << 20),
        name="solve",
    )(place, gathered, first, crossed)
    swapped = exchange(solved, "row")
    near, near_part, outer_rows, second, far = pl.pallas_call(
        late_kernel,
        out_shape=brought,
        in_specs=[SMEM_SPEC, ANY_SPEC] + [HBM_SPEC] * 3 + [VMEM_SPEC] * 6,
        out_specs=(VMEM_SPEC,) * 5,
        scratch_shapes=[pltpu.SemaphoreType.DMA((5,))],
        input_output_aliases={order + 6: order for order in range(5)},
        compiler_params=pltpu.CompilerParams(vmem_limit_bytes=4 << 20),
        cost_estimate=pl.CostEstimate(
            flops=cells * points * loads, bytes_accessed=6 << 20, transcendentals=0
        ),
        name="late",
    )(place, solved, whole_map, data, operator, first, near, *others)
    outputs = (
        jax.ShapeDtypeStruct((boxes, cells, loads), BF16),
        jax.ShapeDtypeStruct((boxes, 3, local, 2 * outer), F32),
    )

    def scratch(pieces):
        return [
            pltpu.VMEM((points - points // 2, loads), BF16),
            pltpu.VMEM((cells, loads), BF16),
            pltpu.VMEM((3, local, 2 * outer), F32),
            pltpu.SemaphoreType.DMA((pieces + 1,)),
        ]

    far_part, *made = pl.pallas_call(
        middle_kernel,
        out_shape=(part,) + outputs,
        in_specs=[SMEM_SPEC] + [VMEM_SPEC] * 8,
        out_specs=(VMEM_SPEC, ANY_SPEC, ANY_SPEC),
        scratch_shapes=scratch(8),
        compiler_params=pltpu.CompilerParams(vmem_limit_bytes=10 << 20),
        cost_estimate=pl.CostEstimate(
            flops=2 * cells * points * loads, bytes_accessed=6 << 20, transcendentals=0
        ),
        name="middle",
    )(place, gathered, outer_rows, solved, first, second, near, far, near_part)
    interior_field, parent_map = pl.pallas_call(
        field_kernel,
        out_shape=outputs,
        in_specs=[SMEM_SPEC] + [VMEM_SPEC] * 6 + [ANY_SPEC] * 2,
        out_specs=(ANY_SPEC, ANY_SPEC),
        scratch_shapes=scratch(8),
        input_output_aliases={7: 0, 8: 1},
        compiler_params=pltpu.CompilerParams(vmem_limit_bytes=10 << 20),
        name="field",
    )(place, gathered, outer_rows, swapped, second, far, far_part, *made)
    return (parent_map, interior_field)


def solution(mesh):
    in_specs = (P("box", None, "row", None), P("box", None, None, None), P("box", "row", None))
    out_specs = (P("box", None, "row", None), P("box", "row", None))
    return jax.shard_map(
        per_device, mesh=mesh, in_specs=in_specs, out_specs=out_specs, check_vma=False
    )
```

```python
import jax
import jax.numpy as jnp
from jax import lax
from jax.experimental import pallas as pl
from jax.experimental.pallas import tpu as pltpu
from jax.sharding import PartitionSpec as P

F32 = jnp.float32
BF16 = jnp.bfloat16
REMAINDER = 2.0**-27
SURE_DOUBLINGS = 4
MOST_DOUBLINGS = 40

SMEM_SPEC = pl.BlockSpec(memory_space=pltpu.SMEM)
VMEM_SPEC = pl.BlockSpec(memory_space=pltpu.VMEM)
HBM_SPEC = pl.BlockSpec(memory_space=pltpu.HBM)
ANY_SPEC = pl.BlockSpec(memory_space=pl.ANY)


def exchange(value, axis):
    pairs = [(source, source ^ 1) for source in range(lax.axis_size(axis))]
    return lax.ppermute(value, axis, pairs)


def in_hbm(value):
    return pltpu.with_memory_space_constraint(value, pltpu.HBM)


def dot(left, right, precision=None):
    return jnp.dot(left, right, precision=precision, preferred_element_type=F32)


def split(value, count):
    pieces = []
    for _ in range(count):
        piece = value.astype(BF16)
        pieces.append(piece)
        value = value - piece.astype(F32)
    return pieces


def split_dot(left, right):
    high, low = split(left, 2)
    right_high, right_low = split(right, 2)
    both = dot(jnp.concatenate([high, low], axis=0), right_high)
    rows = left.shape[0]
    return both[:rows] + (both[rows:] + dot(high, right_low))


def full_dot(left, right):
    return dot(left, right, lax.Precision.HIGHEST)


def start_copies(copies):
    for copy in copies:
        copy.start()


def finish_copies(copies):
    for copy in copies:
        copy.wait()


def start_kernel(map_ref, rows_ref, arrived):
    copy = pltpu.make_async_copy(map_ref.at[:, 3], rows_ref, arrived.at[0])
    copy.start()
    copy.wait()


def far_copies(mine, map_ref, data_ref, operator_ref, outer_ref, second_ref, far_ref, arrived):
    return (
        pltpu.make_async_copy(operator_ref.at[1 - mine], far_ref, arrived.at[2]),
        pltpu.make_async_copy(data_ref.at[1 - mine], second_ref, arrived.at[3]),
        pltpu.make_async_copy(map_ref.at[:, pl.ds(0, 3)], outer_ref, arrived.at[4]),
    )


def first_product(first_ref, near_ref, partial_ref):
    depth = near_ref.shape[1] // 2
    partial_ref[...] = dot(near_ref[:, :depth], first_ref[:depth])


def early_kernel(
    place_ref,
    rows_ref,
    map_ref,
    data_ref,
    operator_ref,
    first_ref,
    near_ref,
    partial_ref,
    outer_ref,
    second_ref,
    far_ref,
    arrived,
):
    mine = place_ref[0] & 1
    level = place_ref[0] // 4
    data_copy = pltpu.make_async_copy(data_ref.at[mine], first_ref, arrived.at[0])
    near_copy = pltpu.make_async_copy(operator_ref.at[mine], near_ref, arrived.at[1])

    @pl.when(level == 0)
    def _():
        copies = far_copies(
            mine, map_ref, data_ref, operator_ref, outer_ref, second_ref, far_ref, arrived
        )
        start_copies((data_copy, near_copy) + copies)
        finish_copies((data_copy, near_copy))
        first_product(first_ref, near_ref, partial_ref)
        finish_copies(copies)

    @pl.when(level == 1)
    def _():
        start_copies((data_copy, near_copy))
        finish_copies((data_copy, near_copy))

    @pl.when(level == 2)
    def _():
        data_copy.start()
        data_copy.wait()


def late_kernel(place_ref, solved_ref, map_ref, data_ref, operator_ref, first_ref, *refs):
    near_ref, partial_ref, outer_ref, second_ref, far_ref, arrived = refs[5:]
    mine = place_ref[0] & 1
    level = place_ref[0] // 4
    copies = far_copies(
        mine, map_ref, data_ref, operator_ref, outer_ref, second_ref, far_ref, arrived
    )

    @pl.when(level == 1)
    def _():
        start_copies(copies)
        first_product(first_ref, near_ref, partial_ref)
        finish_copies(copies)

    @pl.when(level == 2)
    def _():
        near_copy = pltpu.make_async_copy(operator_ref.at[mine], near_ref, arrived.at[1])
        start_copies((near_copy,) + copies)
        near_copy.wait()
        first_product(first_ref, near_ref, partial_ref)
        finish_copies(copies)


def solve_kernel(
    place_ref,
    gathered_ref,
    own_ref,
    other_ref,
    solved_ref,
    sums,
    power_ref,
    terms_ref,
):
    mine = place_ref[0] & 1
    edge = sums.shape[0]
    outer, loads = own_ref.shape
    shared = gathered_ref[:, mine, :, :edge].reshape(edge, edge)
    row = lax.broadcasted_iota(jnp.int32, (edge, edge), 0)
    column = lax.broadcasted_iota(jnp.int32, (edge, edge), 1)
    diagonal = row == column
    kept = jnp.where(diagonal, shared, 0.0)
    scale = 1.0 / jnp.sum(kept, axis=1, keepdims=True)
    right_scale = 1.0 / jnp.sum(kept, axis=0, keepdims=True)
    power = jnp.where(diagonal, 0.0, -shared) * scale
    size = jnp.sum(jnp.abs(power), axis=1, keepdims=True)
    norm = jnp.max(size, axis=0, keepdims=True)[0, 0]

    coupling = gathered_ref[:, mine, :, edge:].reshape(edge, 2 * outer)
    pieces = jnp.concatenate(split(coupling, 2), axis=0)
    block = 2 * edge
    mixed = jnp.concatenate([own_ref[block:], other_ref[:edge]], axis=0)
    parts = dot(pieces[:, :block], own_ref[:block])
    parts += dot(pieces[:, block : 2 * block], mixed)
    parts += dot(pieces[:, 2 * block :], other_ref[edge:])
    terms = parts[:edge] + parts[edge:]

    total = jnp.where(diagonal, 1.0, power)
    power = split_dot(power, power)
    for _ in range(SURE_DOUBLINGS - 1):
        both = split_dot(jnp.concatenate([total, power], axis=0), power)
        total = total + both[:edge]
        power = both[edge:]
    total = total + split_dot(total, power)
    sums[...] = total
    power_ref[...] = power
    terms_ref[...] = terms

    def hand_out(total, terms):
        inverse = total * right_scale
        solved_ref[:, :loads] = (-split_dot(inverse, terms)).astype(BF16)
        for order, piece in enumerate(split(inverse, 3)):
            solved_ref[:, loads + order * edge : loads + (order + 1) * edge] = piece

    hand_out(total, terms)
    bound = norm
    for _ in range(SURE_DOUBLINGS + 1):
        bound = bound * bound

    @pl.when(bound > REMAINDER)
    def _():
        last = power_ref[...]
        power_ref[...] = full_dot(last, last)

        def more(carry):
            left, count = carry
            return jnp.logical_and(left > REMAINDER, count < MOST_DOUBLINGS)

        def double(carry):
            left, count = carry
            held = power_ref[...]
            both = full_dot(jnp.concatenate([sums[...], held], axis=0), held)
            sums[...] = sums[...] + both[:edge]
            power_ref[...] = both[edge:]
            return left * left, count + 1

        lax.while_loop(more, double, (bound, jnp.int32(0)))
        hand_out(sums[...], terms_ref[...])


def parent_rows(place_ref, gathered_ref, outer_ref, solved_ref, box, loads):
    edge = solved_ref.shape[0]
    outer = 3 * edge
    inverse = jnp.zeros((edge, edge), F32)
    for order in (2, 1, 0):
        inverse = inverse + solved_ref[:, loads + order * edge : loads + (order + 1) * edge].astype(F32)
    rows = outer_ref[box].reshape(-1, 4 * edge)
    weights = split_dot(rows[:, outer:], inverse)
    coupling = gathered_ref[:, box, :, edge:].reshape(edge, 2 * outer)
    change = split_dot(weights, coupling)
    own = rows[:, :outer] - change[:, :outer]
    other = -change[:, outer:]
    is_alpha = (place_ref[0] & 2) == 0
    left = jnp.where(is_alpha, own, other)
    right = jnp.where(is_alpha, other, own)
    return jnp.concatenate([left, right], axis=1).reshape(3, -1, 2 * outer)


def finish_field(box, edge_ref, data_ref, operator_ref, part_ref, field_ref, pressure, finished, left):
    outer = data_ref.shape[0]
    cells, points = operator_ref.shape
    depth = points // 2
    loads = data_ref.shape[1]
    pieces = left.shape[0] - 1
    chunk = cells // pieces
    pressure[: outer - depth] = data_ref[depth:]
    pressure[outer - depth :] = edge_ref[:, :loads]
    writes = []
    for order in range(pieces):
        cut = slice(order * chunk, (order + 1) * chunk)
        total = part_ref[cut] + dot(operator_ref[cut, depth:], pressure[...])
        finished[cut] = total.astype(BF16)
        copy = pltpu.make_async_copy(finished.at[cut], field_ref.at[box, cut], left.at[order])
        copy.start()
        writes.append(copy)
    return writes


def finish_parent(place_ref, gathered_ref, outer_ref, edge_ref, box, loads, parent_ref, parent, left):
    parent[...] = parent_rows(place_ref, gathered_ref, outer_ref, edge_ref, box, loads)
    copy = pltpu.make_async_copy(parent, parent_ref.at[box], left.at[left.shape[0] - 1])
    copy.start()
    return [copy]


def middle_kernel(
    place_ref,
    gathered_ref,
    outer_ref,
    solved_ref,
    first_ref,
    second_ref,
    near_ref,
    far_ref,
    near_part_ref,
    far_part_ref,
    field_ref,
    parent_ref,
    pressure,
    finished,
    parent,
    left,
):
    mine = place_ref[0] & 1
    loads = first_ref.shape[1]
    depth = far_ref.shape[1] // 2
    writes = finish_field(
        mine, solved_ref, first_ref, near_ref, near_part_ref, field_ref, pressure, finished, left
    )
    writes += finish_parent(
        place_ref, gathered_ref, outer_ref, solved_ref, mine, loads, parent_ref, parent, left
    )
    far_part_ref[...] = dot(far_ref[:, :depth], second_ref[:depth])
    finish_copies(writes)


def field_kernel(
    place_ref,
    gathered_ref,
    outer_ref,
    swapped_ref,
    second_ref,
    far_ref,
    far_part_ref,
    made_field_ref,
    made_parent_ref,
    field_ref,
    parent_ref,
    pressure,
    finished,
    parent,
    left,
):
    other = 1 - (place_ref[0] & 1)
    loads = second_ref.shape[1]
    writes = finish_field(
        other, swapped_ref, second_ref, far_ref, far_part_ref, field_ref, pressure, finished, left
    )
    writes += finish_parent(
        place_ref, gathered_ref, outer_ref, swapped_ref, other, loads, parent_ref, parent, left
    )
    finish_copies(writes)


def per_device(dtn_map, boundary_data, solution_op):
    boxes, _, local, points = dtn_map.shape
    edge = boundary_data.shape[2]
    loads = boundary_data.shape[3]
    cells = solution_op.shape[1]
    outer = 3 * edge
    side = lax.axis_index("box") & 1
    core = lax.axis_index("row") & 1
    quarter = 4 * lax.axis_index("row") // lax.axis_size("row")
    level = jnp.minimum(quarter, 2)
    place = (4 * level + 2 * side + core).astype(jnp.int32).reshape(1)
    whole_map = in_hbm(dtn_map)
    data = in_hbm(boundary_data.reshape(boxes, outer, loads))
    operator = in_hbm(solution_op)
    half = jax.ShapeDtypeStruct((outer, loads), BF16)
    part = pltpu.VMEM((cells, loads), F32)
    own_rows = pl.pallas_call(
        start_kernel,
        out_shape=jax.ShapeDtypeStruct((boxes, local, points), F32),
        in_specs=[HBM_SPEC],
        out_specs=VMEM_SPEC,
        scratch_shapes=[pltpu.SemaphoreType.DMA((1,))],
        compiler_params=pltpu.CompilerParams(vmem_limit_bytes=4 << 20),
        name="start",
    )(whole_map)
    other_rows = exchange(own_rows, "box")
    brought = (
        pltpu.VMEM((cells, points), BF16),
        part,
        pltpu.VMEM((boxes, 3, local, points), F32),
        pltpu.VMEM((outer, loads), BF16),
        pltpu.VMEM((cells, points), BF16),
    )
    first, near, *others = pl.pallas_call(
        early_kernel,
        out_shape=(half,) + brought,
        in_specs=[SMEM_SPEC, ANY_SPEC, HBM_SPEC, HBM_SPEC, HBM_SPEC],
        out_specs=(VMEM_SPEC,) * 6,
        scratch_shapes=[pltpu.SemaphoreType.DMA((5,))],
        compiler_params=pltpu.CompilerParams(vmem_limit_bytes=4 << 20),
        cost_estimate=pl.CostEstimate(
            flops=cells * points * loads, bytes_accessed=6 << 20, transcendentals=0
        ),
        name="early",
    )(place, own_rows, whole_map, data, operator)
    crossed = exchange(first, "box")
    other_rows, near = lax.optimization_barrier((other_rows, near))
    packed = jnp.concatenate(
        [
            own_rows[:, :, outer:] + other_rows[:, :, outer:],
            own_rows[:, :, :outer],
            other_rows[:, :, :outer],
        ],
        axis=2,
    )
    gathered = lax.all_gather(packed, "row", axis=0)
    solved = pl.pallas_call(
        solve_kernel,
        out_shape=jax.ShapeDtypeStruct((edge, loads + 3 * edge), BF16),
        in_specs=[SMEM_SPEC] + [VMEM_SPEC] * 3,
        out_specs=VMEM_SPEC,
        scratch_shapes=[
            pltpu.VMEM((edge, edge), F32),
            pltpu.VMEM((edge, edge), F32),
            pltpu.VMEM((edge, loads), F32),
        ],
        compiler_params=pltpu.CompilerParams(vmem_limit_bytes=12 << 20),
        name="solve",
    )(place, gathered, first, crossed)
    swapped = exchange(solved, "row")
    near, near_part, outer_rows, second, far = pl.pallas_call(
        late_kernel,
        out_shape=brought,
        in_specs=[SMEM_SPEC, ANY_SPEC] + [HBM_SPEC] * 3 + [VMEM_SPEC] * 6,
        out_specs=(VMEM_SPEC,) * 5,
        scratch_shapes=[pltpu.SemaphoreType.DMA((5,))],
        input_output_aliases={order + 6: order for order in range(5)},
        compiler_params=pltpu.CompilerParams(vmem_limit_bytes=4 << 20),
        cost_estimate=pl.CostEstimate(
            flops=cells * points * loads, bytes_accessed=6 << 20, transcendentals=0
        ),
        name="late",
    )(place, solved, whole_map, data, operator, first, near, *others)
    outputs = (
        jax.ShapeDtypeStruct((boxes, cells, loads), BF16),
        jax.ShapeDtypeStruct((boxes, 3, local, 2 * outer), F32),
    )

    def scratch(pieces):
        return [
            pltpu.VMEM((points - points // 2, loads), BF16),
            pltpu.VMEM((cells, loads), BF16),
            pltpu.VMEM((3, local, 2 * outer), F32),
            pltpu.SemaphoreType.DMA((pieces + 1,)),
        ]

    far_part, *made = pl.pallas_call(
        middle_kernel,
        out_shape=(part,) + outputs,
        in_specs=[SMEM_SPEC] + [VMEM_SPEC] * 8,
        out_specs=(VMEM_SPEC, ANY_SPEC, ANY_SPEC),
        scratch_shapes=scratch(8),
        compiler_params=pltpu.CompilerParams(vmem_limit_bytes=10 << 20),
        cost_estimate=pl.CostEstimate(
            flops=2 * cells * points * loads, bytes_accessed=6 << 20, transcendentals=0
        ),
        name="middle",
    )(place, gathered, outer_rows, solved, first, second, near, far, near_part)
    interior_field, parent_map = pl.pallas_call(
        field_kernel,
        out_shape=outputs,
        in_specs=[SMEM_SPEC] + [VMEM_SPEC] * 6 + [ANY_SPEC] * 2,
        out_specs=(ANY_SPEC, ANY_SPEC),
        scratch_shapes=scratch(8),
        input_output_aliases={7: 0, 8: 1},
        compiler_params=pltpu.CompilerParams(vmem_limit_bytes=10 << 20),
        name="field",
    )(place, gathered, outer_rows, swapped, second, far, far_part, *made)
    return (parent_map, interior_field)


def solution(mesh):
    in_specs = (P("box", None, "row", None), P("box", None, None, None), P("box", "row", None))
    out_specs = (P("box", None, "row", None), P("box", "row", None))
    return jax.shard_map(
        per_device, mesh=mesh, in_specs=in_specs, out_specs=out_specs, check_vma=False
    )
```

```python
import jax
import jax.numpy as jnp
from jax import lax
from jax.experimental import pallas as pl
from jax.experimental.pallas import tpu as pltpu
from jax.sharding import PartitionSpec as P

F32 = jnp.float32
BF16 = jnp.bfloat16
REMAINDER = 2.0**-27
SURE_DOUBLINGS = 4
MOST_DOUBLINGS = 40

SMEM_SPEC = pl.BlockSpec(memory_space=pltpu.SMEM)
VMEM_SPEC = pl.BlockSpec(memory_space=pltpu.VMEM)
HBM_SPEC = pl.BlockSpec(memory_space=pltpu.HBM)
ANY_SPEC = pl.BlockSpec(memory_space=pl.ANY)


def exchange(value, axis):
    pairs = [(source, source ^ 1) for source in range(lax.axis_size(axis))]
    return lax.ppermute(value, axis, pairs)


def in_hbm(value):
    return pltpu.with_memory_space_constraint(value, pltpu.HBM)


def dot(left, right, precision=None):
    return jnp.dot(left, right, precision=precision, preferred_element_type=F32)


def split(value, count):
    pieces = []
    for _ in range(count):
        piece = value.astype(BF16)
        pieces.append(piece)
        value = value - piece.astype(F32)
    return pieces


def split_dot(left, right):
    high, low = split(left, 2)
    right_high, right_low = split(right, 2)
    both = dot(jnp.concatenate([high, low], axis=0), right_high)
    rows = left.shape[0]
    return both[:rows] + (both[rows:] + dot(high, right_low))


def full_dot(left, right):
    return dot(left, right, lax.Precision.HIGHEST)


def start_copies(copies):
    for copy in copies:
        copy.start()


def finish_copies(copies):
    for copy in copies:
        copy.wait()


def start_kernel(map_ref, rows_ref, arrived):
    copy = pltpu.make_async_copy(map_ref.at[:, 3], rows_ref, arrived.at[0])
    copy.start()
    copy.wait()


def far_copies(mine, map_ref, data_ref, operator_ref, outer_ref, second_ref, far_ref, arrived):
    return (
        pltpu.make_async_copy(operator_ref.at[1 - mine], far_ref, arrived.at[2]),
        pltpu.make_async_copy(data_ref.at[1 - mine], second_ref, arrived.at[3]),
        pltpu.make_async_copy(map_ref.at[:, pl.ds(0, 3)], outer_ref, arrived.at[4]),
    )


def first_product(first_ref, near_ref, partial_ref):
    depth = near_ref.shape[1] // 2
    partial_ref[...] = dot(near_ref[:, :depth], first_ref[:depth])


def early_kernel(
    place_ref,
    rows_ref,
    map_ref,
    data_ref,
    operator_ref,
    first_ref,
    near_ref,
    partial_ref,
    outer_ref,
    second_ref,
    far_ref,
    arrived,
):
    mine = place_ref[0] & 1
    level = place_ref[0] // 4
    data_copy = pltpu.make_async_copy(data_ref.at[mine], first_ref, arrived.at[0])
    near_copy = pltpu.make_async_copy(operator_ref.at[mine], near_ref, arrived.at[1])

    @pl.when(level == 0)
    def _():
        copies = far_copies(
            mine, map_ref, data_ref, operator_ref, outer_ref, second_ref, far_ref, arrived
        )
        start_copies((data_copy, near_copy) + copies)
        finish_copies((data_copy, near_copy))
        first_product(first_ref, near_ref, partial_ref)
        finish_copies(copies)

    @pl.when(level == 1)
    def _():
        start_copies((data_copy, near_copy))
        finish_copies((data_copy, near_copy))


def late_kernel(place_ref, solved_ref, map_ref, data_ref, operator_ref, first_ref, *refs):
    near_ref, partial_ref, outer_ref, second_ref, far_ref, arrived = refs[5:]
    mine = place_ref[0] & 1
    level = place_ref[0] // 4
    copies = far_copies(
        mine, map_ref, data_ref, operator_ref, outer_ref, second_ref, far_ref, arrived
    )

    @pl.when(level == 1)
    def _():
        start_copies(copies)
        first_product(first_ref, near_ref, partial_ref)
        finish_copies(copies)


def solve_kernel(
    place_ref,
    gathered_ref,
    own_ref,
    other_ref,
    solved_ref,
    sums,
    power_ref,
    terms_ref,
):
    mine = place_ref[0] & 1
    edge = sums.shape[0]
    outer, loads = own_ref.shape
    shared = gathered_ref[:, mine, :, :edge].reshape(edge, edge)
    row = lax.broadcasted_iota(jnp.int32, (edge, edge), 0)
    column = lax.broadcasted_iota(jnp.int32, (edge, edge), 1)
    diagonal = row == column
    kept = jnp.where(diagonal, shared, 0.0)
    scale = 1.0 / jnp.sum(kept, axis=1, keepdims=True)
    right_scale = 1.0 / jnp.sum(kept, axis=0, keepdims=True)
    power = jnp.where(diagonal, 0.0, -shared) * scale
    size = jnp.sum(jnp.abs(power), axis=1, keepdims=True)
    norm = jnp.max(size, axis=0, keepdims=True)[0, 0]

    coupling = gathered_ref[:, mine, :, edge:].reshape(edge, 2 * outer)
    pieces = jnp.concatenate(split(coupling, 2), axis=0)
    block = 2 * edge
    mixed = jnp.concatenate([own_ref[block:], other_ref[:edge]], axis=0)
    parts = dot(pieces[:, :block], own_ref[:block])
    parts += dot(pieces[:, block : 2 * block], mixed)
    parts += dot(pieces[:, 2 * block :], other_ref[edge:])
    terms = parts[:edge] + parts[edge:]

    total = jnp.where(diagonal, 1.0, power)
    power = split_dot(power, power)
    for _ in range(SURE_DOUBLINGS - 1):
        both = split_dot(jnp.concatenate([total, power], axis=0), power)
        total = total + both[:edge]
        power = both[edge:]
    total = total + split_dot(total, power)
    sums[...] = total
    power_ref[...] = power
    terms_ref[...] = terms

    def hand_out(total, terms):
        inverse = total * right_scale
        solved_ref[:, :loads] = (-split_dot(inverse, terms)).astype(BF16)
        for order, piece in enumerate(split(inverse, 3)):
            solved_ref[:, loads + order * edge : loads + (order + 1) * edge] = piece

    hand_out(total, terms)
    bound = norm
    for _ in range(SURE_DOUBLINGS + 1):
        bound = bound * bound

    @pl.when(bound > REMAINDER)
    def _():
        last = power_ref[...]
        power_ref[...] = full_dot(last, last)

        def more(carry):
            left, count = carry
            return jnp.logical_and(left > REMAINDER, count < MOST_DOUBLINGS)

        def double(carry):
            left, count = carry
            held = power_ref[...]
            both = full_dot(jnp.concatenate([sums[...], held], axis=0), held)
            sums[...] = sums[...] + both[:edge]
            power_ref[...] = both[edge:]
            return left * left, count + 1

        lax.while_loop(more, double, (bound, jnp.int32(0)))
        hand_out(sums[...], terms_ref[...])


def parent_rows(place_ref, gathered_ref, outer_ref, solved_ref, box, loads):
    edge = solved_ref.shape[0]
    outer = 3 * edge
    inverse = jnp.zeros((edge, edge), F32)
    for order in (2, 1, 0):
        inverse = inverse + solved_ref[:, loads + order * edge : loads + (order + 1) * edge].astype(F32)
    rows = outer_ref[box].reshape(-1, 4 * edge)
    weights = split_dot(rows[:, outer:], inverse)
    coupling = gathered_ref[:, box, :, edge:].reshape(edge, 2 * outer)
    change = split_dot(weights, coupling)
    own = rows[:, :outer] - change[:, :outer]
    other = -change[:, outer:]
    is_alpha = (place_ref[0] & 2) == 0
    left = jnp.where(is_alpha, own, other)
    right = jnp.where(is_alpha, other, own)
    return jnp.concatenate([left, right], axis=1).reshape(3, -1, 2 * outer)


def finish_field(box, edge_ref, data_ref, operator_ref, part_ref, field_ref, pressure, finished, left):
    outer = data_ref.shape[0]
    cells, points = operator_ref.shape
    depth = points // 2
    loads = data_ref.shape[1]
    pieces = left.shape[0] - 1
    chunk = cells // pieces
    pressure[: outer - depth] = data_ref[depth:]
    pressure[outer - depth :] = edge_ref[:, :loads]
    writes = []
    for order in range(pieces):
        cut = slice(order * chunk, (order + 1) * chunk)
        total = part_ref[cut] + dot(operator_ref[cut, depth:], pressure[...])
        finished[cut] = total.astype(BF16)
        copy = pltpu.make_async_copy(finished.at[cut], field_ref.at[box, cut], left.at[order])
        copy.start()
        writes.append(copy)
    return writes


def finish_parent(place_ref, gathered_ref, outer_ref, edge_ref, box, loads, parent_ref, parent, left):
    parent[...] = parent_rows(place_ref, gathered_ref, outer_ref, edge_ref, box, loads)
    copy = pltpu.make_async_copy(parent, parent_ref.at[box], left.at[left.shape[0] - 1])
    copy.start()
    return [copy]


def middle_kernel(
    place_ref,
    gathered_ref,
    outer_ref,
    solved_ref,
    first_ref,
    second_ref,
    near_ref,
    far_ref,
    near_part_ref,
    far_part_ref,
    field_ref,
    parent_ref,
    pressure,
    finished,
    parent,
    left,
):
    mine = place_ref[0] & 1
    loads = first_ref.shape[1]
    depth = far_ref.shape[1] // 2
    writes = finish_field(
        mine, solved_ref, first_ref, near_ref, near_part_ref, field_ref, pressure, finished, left
    )
    writes += finish_parent(
        place_ref, gathered_ref, outer_ref, solved_ref, mine, loads, parent_ref, parent, left
    )
    far_part_ref[...] = dot(far_ref[:, :depth], second_ref[:depth])
    finish_copies(writes)


def field_kernel(
    place_ref,
    gathered_ref,
    outer_ref,
    swapped_ref,
    second_ref,
    far_ref,
    far_part_ref,
    made_field_ref,
    made_parent_ref,
    field_ref,
    parent_ref,
    pressure,
    finished,
    parent,
    left,
):
    other = 1 - (place_ref[0] & 1)
    loads = second_ref.shape[1]
    writes = finish_field(
        other, swapped_ref, second_ref, far_ref, far_part_ref, field_ref, pressure, finished, left
    )
    writes += finish_parent(
        place_ref, gathered_ref, outer_ref, swapped_ref, other, loads, parent_ref, parent, left
    )
    finish_copies(writes)


def per_device(dtn_map, boundary_data, solution_op):
    boxes, _, local, points = dtn_map.shape
    edge = boundary_data.shape[2]
    loads = boundary_data.shape[3]
    cells = solution_op.shape[1]
    outer = 3 * edge
    side = lax.axis_index("box") & 1
    core = lax.axis_index("row") & 1
    quarter = 4 * lax.axis_index("row") // lax.axis_size("row")
    level = jnp.minimum(quarter, 1)
    place = (4 * level + 2 * side + core).astype(jnp.int32).reshape(1)
    whole_map = in_hbm(dtn_map)
    data = in_hbm(boundary_data.reshape(boxes, outer, loads))
    operator = in_hbm(solution_op)
    half = jax.ShapeDtypeStruct((outer, loads), BF16)
    part = pltpu.VMEM((cells, loads), F32)
    own_rows = pl.pallas_call(
        start_kernel,
        out_shape=jax.ShapeDtypeStruct((boxes, local, points), F32),
        in_specs=[HBM_SPEC],
        out_specs=VMEM_SPEC,
        scratch_shapes=[pltpu.SemaphoreType.DMA((1,))],
        compiler_params=pltpu.CompilerParams(vmem_limit_bytes=4 << 20),
        name="start",
    )(whole_map)
    other_rows = exchange(own_rows, "box")
    brought = (
        pltpu.VMEM((cells, points), BF16),
        part,
        pltpu.VMEM((boxes, 3, local, points), F32),
        pltpu.VMEM((outer, loads), BF16),
        pltpu.VMEM((cells, points), BF16),
    )
    first, near, *others = pl.pallas_call(
        early_kernel,
        out_shape=(half,) + brought,
        in_specs=[SMEM_SPEC, ANY_SPEC, HBM_SPEC, HBM_SPEC, HBM_SPEC],
        out_specs=(VMEM_SPEC,) * 6,
        scratch_shapes=[pltpu.SemaphoreType.DMA((5,))],
        compiler_params=pltpu.CompilerParams(vmem_limit_bytes=4 << 20),
        cost_estimate=pl.CostEstimate(
            flops=cells * points * loads, bytes_accessed=6 << 20, transcendentals=0
        ),
        name="early",
    )(place, own_rows, whole_map, data, operator)
    crossed = exchange(first, "box")
    other_rows, near = lax.optimization_barrier((other_rows, near))
    packed = jnp.concatenate(
        [
            own_rows[:, :, outer:] + other_rows[:, :, outer:],
            own_rows[:, :, :outer],
            other_rows[:, :, :outer],
        ],
        axis=2,
    )
    gathered = lax.all_gather(packed, "row", axis=0)
    solved = pl.pallas_call(
        solve_kernel,
        out_shape=jax.ShapeDtypeStruct((edge, loads + 3 * edge), BF16),
        in_specs=[SMEM_SPEC] + [VMEM_SPEC] * 3,
        out_specs=VMEM_SPEC,
        scratch_shapes=[
            pltpu.VMEM((edge, edge), F32),
            pltpu.VMEM((edge, edge), F32),
            pltpu.VMEM((edge, loads), F32),
        ],
        compiler_params=pltpu.CompilerParams(vmem_limit_bytes=12 << 20),
        name="solve",
    )(place, gathered, first, crossed)
    swapped = exchange(solved, "row")
    near, near_part, outer_rows, second, far = pl.pallas_call(
        late_kernel,
        out_shape=brought,
        in_specs=[SMEM_SPEC, ANY_SPEC] + [HBM_SPEC] * 3 + [VMEM_SPEC] * 6,
        out_specs=(VMEM_SPEC,) * 5,
        scratch_shapes=[pltpu.SemaphoreType.DMA((5,))],
        input_output_aliases={order + 6: order for order in range(5)},
        compiler_params=pltpu.CompilerParams(vmem_limit_bytes=4 << 20),
        cost_estimate=pl.CostEstimate(
            flops=cells * points * loads, bytes_accessed=6 << 20, transcendentals=0
        ),
        name="late",
    )(place, solved, whole_map, data, operator, first, near, *others)
    outputs = (
        jax.ShapeDtypeStruct((boxes, cells, loads), BF16),
        jax.ShapeDtypeStruct((boxes, 3, local, 2 * outer), F32),
    )

    def scratch(pieces):
        return [
            pltpu.VMEM((points - points // 2, loads), BF16),
            pltpu.VMEM((cells, loads), BF16),
            pltpu.VMEM((3, local, 2 * outer), F32),
            pltpu.SemaphoreType.DMA((pieces + 1,)),
        ]

    far_part, *made = pl.pallas_call(
        middle_kernel,
        out_shape=(part,) + outputs,
        in_specs=[SMEM_SPEC] + [VMEM_SPEC] * 8,
        out_specs=(VMEM_SPEC, ANY_SPEC, ANY_SPEC),
        scratch_shapes=scratch(8),
        compiler_params=pltpu.CompilerParams(vmem_limit_bytes=10 << 20),
        cost_estimate=pl.CostEstimate(
            flops=2 * cells * points * loads, bytes_accessed=6 << 20, transcendentals=0
        ),
        name="middle",
    )(place, gathered, outer_rows, solved, first, second, near, far, near_part)
    interior_field, parent_map = pl.pallas_call(
        field_kernel,
        out_shape=outputs,
        in_specs=[SMEM_SPEC] + [VMEM_SPEC] * 6 + [ANY_SPEC] * 2,
        out_specs=(ANY_SPEC, ANY_SPEC),
        scratch_shapes=scratch(8),
        input_output_aliases={7: 0, 8: 1},
        compiler_params=pltpu.CompilerParams(vmem_limit_bytes=10 << 20),
        name="field",
    )(place, gathered, outer_rows, swapped, second, far, far_part, *made)
    return (parent_map, interior_field)


def solution(mesh):
    in_specs = (P("box", None, "row", None), P("box", None, None, None), P("box", "row", None))
    out_specs = (P("box", None, "row", None), P("box", "row", None))
    return jax.shard_map(
        per_device, mesh=mesh, in_specs=in_specs, out_specs=out_specs, check_vma=False
    )
```

```python
import jax
import jax.numpy as jnp
from jax import lax
from jax.experimental import pallas as pl
from jax.experimental.pallas import tpu as pltpu
from jax.sharding import PartitionSpec as P

F32 = jnp.float32
BF16 = jnp.bfloat16
REMAINDER = 2.0**-27
SURE_DOUBLINGS = 4
MOST_DOUBLINGS = 40

SMEM_SPEC = pl.BlockSpec(memory_space=pltpu.SMEM)
VMEM_SPEC = pl.BlockSpec(memory_space=pltpu.VMEM)
HBM_SPEC = pl.BlockSpec(memory_space=pltpu.HBM)
ANY_SPEC = pl.BlockSpec(memory_space=pl.ANY)


def exchange(value, axis):
    pairs = [(source, source ^ 1) for source in range(lax.axis_size(axis))]
    return lax.ppermute(value, axis, pairs)


def in_hbm(value):
    return pltpu.with_memory_space_constraint(value, pltpu.HBM)


def dot(left, right, precision=None):
    return jnp.dot(left, right, precision=precision, preferred_element_type=F32)


def split(value, count):
    pieces = []
    for _ in range(count):
        piece = value.astype(BF16)
        pieces.append(piece)
        value = value - piece.astype(F32)
    return pieces


def split_dot(left, right):
    high, low = split(left, 2)
    right_high, right_low = split(right, 2)
    both = dot(jnp.concatenate([high, low], axis=0), right_high)
    rows = left.shape[0]
    return both[:rows] + (both[rows:] + dot(high, right_low))


def full_dot(left, right):
    return dot(left, right, lax.Precision.HIGHEST)


def start_copies(copies):
    for copy in copies:
        copy.start()


def finish_copies(copies):
    for copy in copies:
        copy.wait()


def start_kernel(map_ref, rows_ref, arrived):
    copy = pltpu.make_async_copy(map_ref.at[:, 3], rows_ref, arrived.at[0])
    copy.start()
    copy.wait()


def far_copies(mine, map_ref, data_ref, operator_ref, outer_ref, second_ref, far_ref, arrived):
    return (
        pltpu.make_async_copy(operator_ref.at[1 - mine], far_ref, arrived.at[2]),
        pltpu.make_async_copy(data_ref.at[1 - mine], second_ref, arrived.at[3]),
        pltpu.make_async_copy(map_ref.at[:, pl.ds(0, 3)], outer_ref, arrived.at[4]),
    )


def first_product(first_ref, near_ref, partial_ref):
    depth = near_ref.shape[1] // 2
    partial_ref[...] = dot(near_ref[:, :depth], first_ref[:depth])


def early_kernel(
    place_ref,
    rows_ref,
    map_ref,
    data_ref,
    operator_ref,
    first_ref,
    near_ref,
    partial_ref,
    outer_ref,
    second_ref,
    far_ref,
    arrived,
):
    mine = place_ref[0] & 1
    level = place_ref[0] // 4
    data_copy = pltpu.make_async_copy(data_ref.at[mine], first_ref, arrived.at[0])
    near_copy = pltpu.make_async_copy(operator_ref.at[mine], near_ref, arrived.at[1])

    @pl.when(level == 0)
    def _():
        copies = far_copies(
            mine, map_ref, data_ref, operator_ref, outer_ref, second_ref, far_ref, arrived
        )
        start_copies((data_copy, near_copy) + copies)
        finish_copies((data_copy, near_copy))
        first_product(first_ref, near_ref, partial_ref)
        finish_copies(copies)

    @pl.when(level == 1)
    def _():
        start_copies((data_copy, near_copy))
        finish_copies((data_copy, near_copy))


def late_kernel(place_ref, solved_ref, map_ref, data_ref, operator_ref, first_ref, *refs):
    near_ref, partial_ref, outer_ref, second_ref, far_ref, arrived = refs[5:]
    mine = place_ref[0] & 1
    level = place_ref[0] // 4
    copies = far_copies(
        mine, map_ref, data_ref, operator_ref, outer_ref, second_ref, far_ref, arrived
    )

    @pl.when(level == 1)
    def _():
        start_copies(copies)
        first_product(first_ref, near_ref, partial_ref)
        finish_copies(copies)


def solve_kernel(
    place_ref,
    gathered_ref,
    own_ref,
    other_ref,
    solved_ref,
    sums,
    power_ref,
):
    mine = place_ref[0] & 1
    edge = sums.shape[0]
    outer, loads = own_ref.shape
    shared = gathered_ref[:, mine, :, :edge].reshape(edge, edge)
    row = lax.broadcasted_iota(jnp.int32, (edge, edge), 0)
    column = lax.broadcasted_iota(jnp.int32, (edge, edge), 1)
    diagonal = row == column
    kept = jnp.where(diagonal, shared, 0.0)
    scale = 1.0 / jnp.sum(kept, axis=1, keepdims=True)
    right_scale = 1.0 / jnp.sum(kept, axis=0, keepdims=True)
    power = jnp.where(diagonal, 0.0, -shared) * scale
    power_ref[...] = power
    size = jnp.sum(jnp.abs(power), axis=1, keepdims=True)
    norm = jnp.max(size, axis=0, keepdims=True)[0, 0]

    coupling = gathered_ref[:, mine, :, edge:].reshape(edge, 2 * outer)
    pieces = jnp.concatenate(split(coupling, 2), axis=0)
    block = 2 * edge
    mixed = jnp.concatenate([own_ref[block:], other_ref[:edge]], axis=0)
    parts = dot(pieces[:, :block], own_ref[:block])
    parts += dot(pieces[:, block : 2 * block], mixed)
    parts += dot(pieces[:, 2 * block :], other_ref[edge:])
    terms = parts[:edge] + parts[edge:]

    total = jnp.where(diagonal, 1.0, power)
    power = split_dot(power, power)
    for _ in range(SURE_DOUBLINGS - 1):
        both = split_dot(jnp.concatenate([total, power], axis=0), power)
        total = total + both[:edge]
        power = both[edge:]
    total = total + split_dot(total, power)

    def hand_out(inverse, values):
        solved_ref[:, :loads] = (-values).astype(BF16)
        for order, piece in enumerate(split(inverse, 3)):
            solved_ref[:, loads + order * edge : loads + (order + 1) * edge] = piece

    inverse = total * right_scale
    hand_out(inverse, split_dot(inverse, terms))
    bound = norm
    for _ in range(SURE_DOUBLINGS + 1):
        bound = bound * bound

    @pl.when(bound > REMAINDER)
    def _():
        sums[...] = jnp.where(diagonal, 1.0, 0.0)

        def more(carry):
            left, count = carry
            return jnp.logical_and(left > REMAINDER, count < MOST_DOUBLINGS)

        def double(carry):
            left, count = carry
            held = power_ref[...]
            both = full_dot(jnp.concatenate([sums[...], held], axis=0), held)
            sums[...] = sums[...] + both[:edge]
            power_ref[...] = both[edge:]
            return left * left, count + 1

        lax.while_loop(more, double, (norm, jnp.int32(0)))
        fine = dot(jnp.concatenate(split(coupling[:, :outer], 3), axis=0), own_ref[...])
        fine += dot(jnp.concatenate(split(coupling[:, outer:], 3), axis=0), other_ref[...])
        exact = fine[:edge] + (fine[edge : 2 * edge] + fine[2 * edge :])
        inverse = sums[...] * right_scale
        hand_out(inverse, full_dot(inverse, exact))


def parent_rows(place_ref, gathered_ref, outer_ref, solved_ref, box, loads):
    edge = solved_ref.shape[0]
    outer = 3 * edge
    inverse = jnp.zeros((edge, edge), F32)
    for order in (2, 1, 0):
        inverse = inverse + solved_ref[:, loads + order * edge : loads + (order + 1) * edge].astype(F32)
    rows = outer_ref[box].reshape(-1, 4 * edge)
    weights = split_dot(rows[:, outer:], inverse)
    coupling = gathered_ref[:, box, :, edge:].reshape(edge, 2 * outer)
    change = split_dot(weights, coupling)
    own = rows[:, :outer] - change[:, :outer]
    other = -change[:, outer:]
    is_alpha = (place_ref[0] & 2) == 0
    left = jnp.where(is_alpha, own, other)
    right = jnp.where(is_alpha, other, own)
    return jnp.concatenate([left, right], axis=1).reshape(3, -1, 2 * outer)


def finish_field(box, edge_ref, data_ref, operator_ref, part_ref, field_ref, pressure, finished, left):
    outer = data_ref.shape[0]
    cells, points = operator_ref.shape
    depth = points // 2
    loads = data_ref.shape[1]
    pieces = left.shape[0] - 1
    chunk = cells // pieces
    pressure[: outer - depth] = data_ref[depth:]
    pressure[outer - depth :] = edge_ref[:, :loads]
    writes = []
    for order in range(pieces):
        cut = slice(order * chunk, (order + 1) * chunk)
        total = part_ref[cut] + dot(operator_ref[cut, depth:], pressure[...])
        finished[cut] = total.astype(BF16)
        copy = pltpu.make_async_copy(finished.at[cut], field_ref.at[box, cut], left.at[order])
        copy.start()
        writes.append(copy)
    return writes


def finish_parent(place_ref, gathered_ref, outer_ref, edge_ref, box, loads, parent_ref, parent, left):
    parent[...] = parent_rows(place_ref, gathered_ref, outer_ref, edge_ref, box, loads)
    copy = pltpu.make_async_copy(parent, parent_ref.at[box], left.at[left.shape[0] - 1])
    copy.start()
    return [copy]


def middle_kernel(
    place_ref,
    gathered_ref,
    outer_ref,
    solved_ref,
    first_ref,
    second_ref,
    near_ref,
    far_ref,
    near_part_ref,
    far_part_ref,
    field_ref,
    parent_ref,
    pressure,
    finished,
    parent,
    left,
):
    mine = place_ref[0] & 1
    loads = first_ref.shape[1]
    depth = far_ref.shape[1] // 2
    writes = finish_field(
        mine, solved_ref, first_ref, near_ref, near_part_ref, field_ref, pressure, finished, left
    )
    writes += finish_parent(
        place_ref, gathered_ref, outer_ref, solved_ref, mine, loads, parent_ref, parent, left
    )
    far_part_ref[...] = dot(far_ref[:, :depth], second_ref[:depth])
    finish_copies(writes)


def field_kernel(
    place_ref,
    gathered_ref,
    outer_ref,
    swapped_ref,
    second_ref,
    far_ref,
    far_part_ref,
    made_field_ref,
    made_parent_ref,
    field_ref,
    parent_ref,
    pressure,
    finished,
    parent,
    left,
):
    other = 1 - (place_ref[0] & 1)
    loads = second_ref.shape[1]
    writes = finish_field(
        other, swapped_ref, second_ref, far_ref, far_part_ref, field_ref, pressure, finished, left
    )
    writes += finish_parent(
        place_ref, gathered_ref, outer_ref, swapped_ref, other, loads, parent_ref, parent, left
    )
    finish_copies(writes)


def per_device(dtn_map, boundary_data, solution_op):
    boxes, _, local, points = dtn_map.shape
    edge = boundary_data.shape[2]
    loads = boundary_data.shape[3]
    cells = solution_op.shape[1]
    outer = 3 * edge
    side = lax.axis_index("box") & 1
    core = lax.axis_index("row") & 1
    quarter = 4 * lax.axis_index("row") // lax.axis_size("row")
    level = jnp.minimum(quarter, 1)
    place = (4 * level + 2 * side + core).astype(jnp.int32).reshape(1)
    whole_map = in_hbm(dtn_map)
    data = in_hbm(boundary_data.reshape(boxes, outer, loads))
    operator = in_hbm(solution_op)
    half = jax.ShapeDtypeStruct((outer, loads), BF16)
    part = pltpu.VMEM((cells, loads), F32)
    own_rows = pl.pallas_call(
        start_kernel,
        out_shape=jax.ShapeDtypeStruct((boxes, local, points), F32),
        in_specs=[HBM_SPEC],
        out_specs=VMEM_SPEC,
        scratch_shapes=[pltpu.SemaphoreType.DMA((1,))],
        compiler_params=pltpu.CompilerParams(vmem_limit_bytes=4 << 20),
        name="start",
    )(whole_map)
    other_rows = exchange(own_rows, "box")
    brought = (
        pltpu.VMEM((cells, points), BF16),
        part,
        pltpu.VMEM((boxes, 3, local, points), F32),
        pltpu.VMEM((outer, loads), BF16),
        pltpu.VMEM((cells, points), BF16),
    )
    first, near, *others = pl.pallas_call(
        early_kernel,
        out_shape=(half,) + brought,
        in_specs=[SMEM_SPEC, ANY_SPEC, HBM_SPEC, HBM_SPEC, HBM_SPEC],
        out_specs=(VMEM_SPEC,) * 6,
        scratch_shapes=[pltpu.SemaphoreType.DMA((5,))],
        compiler_params=pltpu.CompilerParams(vmem_limit_bytes=4 << 20),
        cost_estimate=pl.CostEstimate(
            flops=cells * points * loads, bytes_accessed=6 << 20, transcendentals=0
        ),
        name="early",
    )(place, own_rows, whole_map, data, operator)
    crossed = exchange(first, "box")
    other_rows, near = lax.optimization_barrier((other_rows, near))
    packed = jnp.concatenate(
        [
            own_rows[:, :, outer:] + other_rows[:, :, outer:],
            own_rows[:, :, :outer],
            other_rows[:, :, :outer],
        ],
        axis=2,
    )
    gathered = lax.all_gather(packed, "row", axis=0)
    solved = pl.pallas_call(
        solve_kernel,
        out_shape=jax.ShapeDtypeStruct((edge, loads + 3 * edge), BF16),
        in_specs=[SMEM_SPEC] + [VMEM_SPEC] * 3,
        out_specs=VMEM_SPEC,
        scratch_shapes=[
            pltpu.VMEM((edge, edge), F32),
            pltpu.VMEM((edge, edge), F32),
        ],
        compiler_params=pltpu.CompilerParams(vmem_limit_bytes=12 << 20),
        name="solve",
    )(place, gathered, first, crossed)
    swapped = exchange(solved, "row")
    near, near_part, outer_rows, second, far = pl.pallas_call(
        late_kernel,
        out_shape=brought,
        in_specs=[SMEM_SPEC, ANY_SPEC] + [HBM_SPEC] * 3 + [VMEM_SPEC] * 6,
        out_specs=(VMEM_SPEC,) * 5,
        scratch_shapes=[pltpu.SemaphoreType.DMA((5,))],
        input_output_aliases={order + 6: order for order in range(5)},
        compiler_params=pltpu.CompilerParams(vmem_limit_bytes=4 << 20),
        cost_estimate=pl.CostEstimate(
            flops=cells * points * loads, bytes_accessed=6 << 20, transcendentals=0
        ),
        name="late",
    )(place, solved, whole_map, data, operator, first, near, *others)
    outputs = (
        jax.ShapeDtypeStruct((boxes, cells, loads), BF16),
        jax.ShapeDtypeStruct((boxes, 3, local, 2 * outer), F32),
    )

    def scratch(pieces):
        return [
            pltpu.VMEM((points - points // 2, loads), BF16),
            pltpu.VMEM((cells, loads), BF16),
            pltpu.VMEM((3, local, 2 * outer), F32),
            pltpu.SemaphoreType.DMA((pieces + 1,)),
        ]

    far_part, *made = pl.pallas_call(
        middle_kernel,
        out_shape=(part,) + outputs,
        in_specs=[SMEM_SPEC] + [VMEM_SPEC] * 8,
        out_specs=(VMEM_SPEC, ANY_SPEC, ANY_SPEC),
        scratch_shapes=scratch(8),
        compiler_params=pltpu.CompilerParams(vmem_limit_bytes=10 << 20),
        cost_estimate=pl.CostEstimate(
            flops=2 * cells * points * loads, bytes_accessed=6 << 20, transcendentals=0
        ),
        name="middle",
    )(place, gathered, outer_rows, solved, first, second, near, far, near_part)
    interior_field, parent_map = pl.pallas_call(
        field_kernel,
        out_shape=outputs,
        in_specs=[SMEM_SPEC] + [VMEM_SPEC] * 6 + [ANY_SPEC] * 2,
        out_specs=(ANY_SPEC, ANY_SPEC),
        scratch_shapes=scratch(8),
        input_output_aliases={7: 0, 8: 1},
        compiler_params=pltpu.CompilerParams(vmem_limit_bytes=10 << 20),
        name="field",
    )(place, gathered, outer_rows, swapped, second, far, far_part, *made)
    return (parent_map, interior_field)


def solution(mesh):
    in_specs = (P("box", None, "row", None), P("box", None, None, None), P("box", "row", None))
    out_specs = (P("box", None, "row", None), P("box", "row", None))
    return jax.shard_map(
        per_device, mesh=mesh, in_specs=in_specs, out_specs=out_specs, check_vma=False
    )
```

```python
import jax
import jax.numpy as jnp
from jax import lax
from jax.experimental import pallas as pl
from jax.experimental.pallas import tpu as pltpu
from jax.sharding import PartitionSpec as P

F32 = jnp.float32
BF16 = jnp.bfloat16
REMAINDER = 2.0**-27
SURE_DOUBLINGS = 4
MOST_DOUBLINGS = 40

SMEM_SPEC = pl.BlockSpec(memory_space=pltpu.SMEM)
VMEM_SPEC = pl.BlockSpec(memory_space=pltpu.VMEM)
HBM_SPEC = pl.BlockSpec(memory_space=pltpu.HBM)
ANY_SPEC = pl.BlockSpec(memory_space=pl.ANY)


def exchange(value, axis):
    pairs = [(source, source ^ 1) for source in range(lax.axis_size(axis))]
    return lax.ppermute(value, axis, pairs)


def in_hbm(value):
    return pltpu.with_memory_space_constraint(value, pltpu.HBM)


def dot(left, right, precision=None):
    return jnp.dot(left, right, precision=precision, preferred_element_type=F32)


def split(value, count):
    pieces = []
    for _ in range(count):
        piece = value.astype(BF16)
        pieces.append(piece)
        value = value - piece.astype(F32)
    return pieces


def split_dot(left, right):
    high, low = split(left, 2)
    right_high, right_low = split(right, 2)
    both = dot(jnp.concatenate([high, low], axis=0), right_high)
    rows = left.shape[0]
    return both[:rows] + (both[rows:] + dot(high, right_low))


def full_dot(left, right):
    return dot(left, right, lax.Precision.HIGHEST)


def start_copies(copies):
    for copy in copies:
        copy.start()


def finish_copies(copies):
    for copy in copies:
        copy.wait()


def start_kernel(map_ref, rows_ref, arrived):
    copy = pltpu.make_async_copy(map_ref.at[:, 3], rows_ref, arrived.at[0])
    copy.start()
    copy.wait()


def far_copies(mine, map_ref, data_ref, operator_ref, outer_ref, second_ref, far_ref, arrived):
    return (
        pltpu.make_async_copy(operator_ref.at[1 - mine], far_ref, arrived.at[2]),
        pltpu.make_async_copy(data_ref.at[1 - mine], second_ref, arrived.at[3]),
        pltpu.make_async_copy(map_ref.at[:, pl.ds(0, 3)], outer_ref, arrived.at[4]),
    )


def first_product(first_ref, near_ref, partial_ref):
    depth = near_ref.shape[1] // 2
    partial_ref[...] = dot(near_ref[:, :depth], first_ref[:depth])


def early_kernel(
    place_ref,
    rows_ref,
    map_ref,
    data_ref,
    operator_ref,
    first_ref,
    near_ref,
    partial_ref,
    outer_ref,
    second_ref,
    far_ref,
    arrived,
):
    mine = place_ref[0] & 1
    level = place_ref[0] // 4
    data_copy = pltpu.make_async_copy(data_ref.at[mine], first_ref, arrived.at[0])
    near_copy = pltpu.make_async_copy(operator_ref.at[mine], near_ref, arrived.at[1])

    @pl.when(level == 0)
    def _():
        copies = far_copies(
            mine, map_ref, data_ref, operator_ref, outer_ref, second_ref, far_ref, arrived
        )
        start_copies((data_copy, near_copy) + copies)
        finish_copies((data_copy, near_copy))
        first_product(first_ref, near_ref, partial_ref)
        finish_copies(copies)

    @pl.when(level == 1)
    def _():
        copies = far_copies(
            mine, map_ref, data_ref, operator_ref, outer_ref, second_ref, far_ref, arrived
        )
        start_copies((data_copy, near_copy) + copies[1:])
        finish_copies((data_copy, near_copy) + copies[1:])


def late_kernel(place_ref, solved_ref, map_ref, data_ref, operator_ref, first_ref, *refs):
    near_ref, partial_ref, outer_ref, second_ref, far_ref, arrived = refs[5:]
    mine = place_ref[0] & 1
    level = place_ref[0] // 4
    copies = far_copies(
        mine, map_ref, data_ref, operator_ref, outer_ref, second_ref, far_ref, arrived
    )

    @pl.when(level == 1)
    def _():
        copies[0].start()
        first_product(first_ref, near_ref, partial_ref)
        copies[0].wait()


def solve_kernel(
    place_ref,
    gathered_ref,
    own_ref,
    other_ref,
    solved_ref,
    sums,
    power_ref,
):
    mine = place_ref[0] & 1
    edge = sums.shape[0]
    outer, loads = own_ref.shape
    shared = gathered_ref[:, mine, :, :edge].reshape(edge, edge)
    row = lax.broadcasted_iota(jnp.int32, (edge, edge), 0)
    column = lax.broadcasted_iota(jnp.int32, (edge, edge), 1)
    diagonal = row == column
    kept = jnp.where(diagonal, shared, 0.0)
    scale = 1.0 / jnp.sum(kept, axis=1, keepdims=True)
    right_scale = 1.0 / jnp.sum(kept, axis=0, keepdims=True)
    power = jnp.where(diagonal, 0.0, -shared) * scale
    power_ref[...] = power
    size = jnp.sum(jnp.abs(power), axis=1, keepdims=True)
    norm = jnp.max(size, axis=0, keepdims=True)[0, 0]

    coupling = gathered_ref[:, mine, :, edge:].reshape(edge, 2 * outer)
    pieces = jnp.concatenate(split(coupling, 2), axis=0)
    block = 2 * edge
    mixed = jnp.concatenate([own_ref[block:], other_ref[:edge]], axis=0)
    parts = dot(pieces[:, :block], own_ref[:block])
    parts += dot(pieces[:, block : 2 * block], mixed)
    parts += dot(pieces[:, 2 * block :], other_ref[edge:])
    terms = parts[:edge] + parts[edge:]

    total = jnp.where(diagonal, 1.0, power)
    power = split_dot(power, power)
    for _ in range(SURE_DOUBLINGS - 1):
        both = split_dot(jnp.concatenate([total, power], axis=0), power)
        total = total + both[:edge]
        power = both[edge:]
    total = total + split_dot(total, power)

    def hand_out(inverse, values):
        solved_ref[:, :loads] = (-values).astype(BF16)
        for order, piece in enumerate(split(inverse, 3)):
            solved_ref[:, loads + order * edge : loads + (order + 1) * edge] = piece

    inverse = total * right_scale
    hand_out(inverse, split_dot(inverse, terms))
    bound = norm
    for _ in range(SURE_DOUBLINGS + 1):
        bound = bound * bound

    @pl.when(bound > REMAINDER)
    def _():
        sums[...] = jnp.where(diagonal, 1.0, 0.0)

        def more(carry):
            left, count = carry
            return jnp.logical_and(left > REMAINDER, count < MOST_DOUBLINGS)

        def double(carry):
            left, count = carry
            held = power_ref[...]
            both = full_dot(jnp.concatenate([sums[...], held], axis=0), held)
            sums[...] = sums[...] + both[:edge]
            power_ref[...] = both[edge:]
            return left * left, count + 1

        lax.while_loop(more, double, (norm, jnp.int32(0)))
        fine = dot(jnp.concatenate(split(coupling[:, :outer], 3), axis=0), own_ref[...])
        fine += dot(jnp.concatenate(split(coupling[:, outer:], 3), axis=0), other_ref[...])
        exact = fine[:edge] + (fine[edge : 2 * edge] + fine[2 * edge :])
        inverse = sums[...] * right_scale
        hand_out(inverse, full_dot(inverse, exact))


def parent_rows(place_ref, gathered_ref, outer_ref, solved_ref, box, loads):
    edge = solved_ref.shape[0]
    outer = 3 * edge
    inverse = jnp.zeros((edge, edge), F32)
    for order in (2, 1, 0):
        inverse = inverse + solved_ref[:, loads + order * edge : loads + (order + 1) * edge].astype(F32)
    rows = outer_ref[box].reshape(-1, 4 * edge)
    weights = split_dot(rows[:, outer:], inverse)
    coupling = gathered_ref[:, box, :, edge:].reshape(edge, 2 * outer)
    change = split_dot(weights, coupling)
    own = rows[:, :outer] - change[:, :outer]
    other = -change[:, outer:]
    is_alpha = (place_ref[0] & 2) == 0
    left = jnp.where(is_alpha, own, other)
    right = jnp.where(is_alpha, other, own)
    return jnp.concatenate([left, right], axis=1).reshape(3, -1, 2 * outer)


def finish_field(box, edge_ref, data_ref, operator_ref, part_ref, field_ref, pressure, finished, left):
    outer = data_ref.shape[0]
    cells, points = operator_ref.shape
    depth = points // 2
    loads = data_ref.shape[1]
    pieces = left.shape[0] - 1
    chunk = cells // pieces
    pressure[: outer - depth] = data_ref[depth:]
    pressure[outer - depth :] = edge_ref[:, :loads]
    writes = []
    for order in range(pieces):
        cut = slice(order * chunk, (order + 1) * chunk)
        total = part_ref[cut] + dot(operator_ref[cut, depth:], pressure[...])
        finished[cut] = total.astype(BF16)
        copy = pltpu.make_async_copy(finished.at[cut], field_ref.at[box, cut], left.at[order])
        copy.start()
        writes.append(copy)
    return writes


def finish_parent(place_ref, gathered_ref, outer_ref, edge_ref, box, loads, parent_ref, parent, left):
    parent[...] = parent_rows(place_ref, gathered_ref, outer_ref, edge_ref, box, loads)
    copy = pltpu.make_async_copy(parent, parent_ref.at[box], left.at[left.shape[0] - 1])
    copy.start()
    return [copy]


def middle_kernel(
    place_ref,
    gathered_ref,
    outer_ref,
    solved_ref,
    first_ref,
    second_ref,
    near_ref,
    far_ref,
    near_part_ref,
    far_part_ref,
    field_ref,
    parent_ref,
    pressure,
    finished,
    parent,
    left,
):
    mine = place_ref[0] & 1
    loads = first_ref.shape[1]
    depth = far_ref.shape[1] // 2
    writes = finish_field(
        mine, solved_ref, first_ref, near_ref, near_part_ref, field_ref, pressure, finished, left
    )
    writes += finish_parent(
        place_ref, gathered_ref, outer_ref, solved_ref, mine, loads, parent_ref, parent, left
    )
    far_part_ref[...] = dot(far_ref[:, :depth], second_ref[:depth])
    finish_copies(writes)


def field_kernel(
    place_ref,
    gathered_ref,
    outer_ref,
    swapped_ref,
    second_ref,
    far_ref,
    far_part_ref,
    made_field_ref,
    made_parent_ref,
    field_ref,
    parent_ref,
    pressure,
    finished,
    parent,
    left,
):
    other = 1 - (place_ref[0] & 1)
    loads = second_ref.shape[1]
    writes = finish_field(
        other, swapped_ref, second_ref, far_ref, far_part_ref, field_ref, pressure, finished, left
    )
    writes += finish_parent(
        place_ref, gathered_ref, outer_ref, swapped_ref, other, loads, parent_ref, parent, left
    )
    finish_copies(writes)


def per_device(dtn_map, boundary_data, solution_op):
    boxes, _, local, points = dtn_map.shape
    edge = boundary_data.shape[2]
    loads = boundary_data.shape[3]
    cells = solution_op.shape[1]
    outer = 3 * edge
    side = lax.axis_index("box") & 1
    core = lax.axis_index("row") & 1
    quarter = 4 * lax.axis_index("row") // lax.axis_size("row")
    level = jnp.minimum(quarter, 1)
    place = (4 * level + 2 * side + core).astype(jnp.int32).reshape(1)
    whole_map = in_hbm(dtn_map)
    data = in_hbm(boundary_data.reshape(boxes, outer, loads))
    operator = in_hbm(solution_op)
    half = jax.ShapeDtypeStruct((outer, loads), BF16)
    part = pltpu.VMEM((cells, loads), F32)
    own_rows = pl.pallas_call(
        start_kernel,
        out_shape=jax.ShapeDtypeStruct((boxes, local, points), F32),
        in_specs=[HBM_SPEC],
        out_specs=VMEM_SPEC,
        scratch_shapes=[pltpu.SemaphoreType.DMA((1,))],
        compiler_params=pltpu.CompilerParams(vmem_limit_bytes=4 << 20),
        name="start",
    )(whole_map)
    other_rows = exchange(own_rows, "box")
    brought = (
        pltpu.VMEM((cells, points), BF16),
        part,
        pltpu.VMEM((boxes, 3, local, points), F32),
        pltpu.VMEM((outer, loads), BF16),
        pltpu.VMEM((cells, points), BF16),
    )
    first, near, *others = pl.pallas_call(
        early_kernel,
        out_shape=(half,) + brought,
        in_specs=[SMEM_SPEC, ANY_SPEC, HBM_SPEC, HBM_SPEC, HBM_SPEC],
        out_specs=(VMEM_SPEC,) * 6,
        scratch_shapes=[pltpu.SemaphoreType.DMA((5,))],
        compiler_params=pltpu.CompilerParams(vmem_limit_bytes=4 << 20),
        cost_estimate=pl.CostEstimate(
            flops=cells * points * loads, bytes_accessed=6 << 20, transcendentals=0
        ),
        name="early",
    )(place, own_rows, whole_map, data, operator)
    crossed = exchange(first, "box")
    other_rows, near = lax.optimization_barrier((other_rows, near))
    packed = jnp.concatenate(
        [
            own_rows[:, :, outer:] + other_rows[:, :, outer:],
            own_rows[:, :, :outer],
            other_rows[:, :, :outer],
        ],
        axis=2,
    )
    gathered = lax.all_gather(packed, "row", axis=0)
    solved = pl.pallas_call(
        solve_kernel,
        out_shape=jax.ShapeDtypeStruct((edge, loads + 3 * edge), BF16),
        in_specs=[SMEM_SPEC] + [VMEM_SPEC] * 3,
        out_specs=VMEM_SPEC,
        scratch_shapes=[
            pltpu.VMEM((edge, edge), F32),
            pltpu.VMEM((edge, edge), F32),
        ],
        compiler_params=pltpu.CompilerParams(vmem_limit_bytes=12 << 20),
        name="solve",
    )(place, gathered, first, crossed)
    swapped = exchange(solved, "row")
    near, near_part, outer_rows, second, far = pl.pallas_call(
        late_kernel,
        out_shape=brought,
        in_specs=[SMEM_SPEC, ANY_SPEC] + [HBM_SPEC] * 3 + [VMEM_SPEC] * 6,
        out_specs=(VMEM_SPEC,) * 5,
        scratch_shapes=[pltpu.SemaphoreType.DMA((5,))],
        input_output_aliases={order + 6: order for order in range(5)},
        compiler_params=pltpu.CompilerParams(vmem_limit_bytes=4 << 20),
        cost_estimate=pl.CostEstimate(
            flops=cells * points * loads, bytes_accessed=6 << 20, transcendentals=0
        ),
        name="late",
    )(place, solved, whole_map, data, operator, first, near, *others)
    outputs = (
        jax.ShapeDtypeStruct((boxes, cells, loads), BF16),
        jax.ShapeDtypeStruct((boxes, 3, local, 2 * outer), F32),
    )

    def scratch(pieces):
        return [
            pltpu.VMEM((points - points // 2, loads), BF16),
            pltpu.VMEM((cells, loads), BF16),
            pltpu.VMEM((3, local, 2 * outer), F32),
            pltpu.SemaphoreType.DMA((pieces + 1,)),
        ]

    far_part, *made = pl.pallas_call(
        middle_kernel,
        out_shape=(part,) + outputs,
        in_specs=[SMEM_SPEC] + [VMEM_SPEC] * 8,
        out_specs=(VMEM_SPEC, ANY_SPEC, ANY_SPEC),
        scratch_shapes=scratch(8),
        compiler_params=pltpu.CompilerParams(vmem_limit_bytes=10 << 20),
        cost_estimate=pl.CostEstimate(
            flops=2 * cells * points * loads, bytes_accessed=6 << 20, transcendentals=0
        ),
        name="middle",
    )(place, gathered, outer_rows, solved, first, second, near, far, near_part)
    interior_field, parent_map = pl.pallas_call(
        field_kernel,
        out_shape=outputs,
        in_specs=[SMEM_SPEC] + [VMEM_SPEC] * 6 + [ANY_SPEC] * 2,
        out_specs=(ANY_SPEC, ANY_SPEC),
        scratch_shapes=scratch(8),
        input_output_aliases={7: 0, 8: 1},
        compiler_params=pltpu.CompilerParams(vmem_limit_bytes=10 << 20),
        name="field",
    )(place, gathered, outer_rows, swapped, second, far, far_part, *made)
    return (parent_map, interior_field)


def solution(mesh):
    in_specs = (P("box", None, "row", None), P("box", None, None, None), P("box", "row", None))
    out_specs = (P("box", None, "row", None), P("box", "row", None))
    return jax.shard_map(
        per_device, mesh=mesh, in_specs=in_specs, out_specs=out_specs, check_vma=False
    )
```
